32 devices in a mesh: slab: 2 (over y), frames: 4 (over z), medoids: 4 (over x, core).
Axes of the slice: x: 2, y: 2, z: 4, core: 2. Of those that a mesh axis runs over, the one named last changes fastest.
Arguments:
- frames: bfloat16 [16384, 512], P(('slab', 'frames')), parts along dimension 0, may hold values from -6 to 6
- medoids: bfloat16 [4, 8192, 512], P('medoids', 'frames'), may hold values from -6 to 6
- tile_ids: int32 [4, 128, 24], P('medoids', ('slab', 'frames')), parts along dimension 1, may hold values from 0 to 63, as said below
- tile_counts: int32 [4, 128], P('medoids', ('slab', 'frames')), parts along dimension 1, may hold values from 1 to 24, as said below
- plan: int32 [128], P('slab'), parts along dimension 0, may hold values from 0 to 63, as said below
Outputs:
- nearest: float32 [16384], P(('slab', 'frames')), parts along dimension 0
- second: float32 [16384], P(('slab', 'frames')), parts along dimension 0
The draws below stay inside these ranges and needn't reach their ends.
There are 2 independent parts, one for each index of `slab`. The reference program is written for one: setup_inputs(seed, part) draws one part's arguments, and reference() takes and returns one part's arrays. A program takes and returns all parts, laid end to end along the dimension named above; an argument that names none is the same for every part. Nothing has to cross between parts.
Inputs may be any that keep to these rules, and one draw needn't show every extreme that they name: plan is a permutation. Of the frame tiles 16 i to 16 i + 15, at most 4 stand at positions 16 j to 16 j + 15 of plan's inverse for one j, and exactly 4 for some j, for every i. `tile_ids`: the 24 entries of one list are distinct; entries at l >= tile_counts[m, g] are ignored. `tile_counts`: the largest value is reached in every draw.
All inputs are finite; a program needn't handle non-finite values.
Results may differ from the reference program's by a relative error of at most 0.0003.
Values may be sent and summed in bfloat16 or wider, within the bound.
No kernel may reach another device: no remote copies, remote signals or barrier semaphores. Data moves between devices by JAX's collectives and lax.ppermute only.
A program may use at most 64 MiB of HBM per device.

```python
import jax
import jax.numpy as jnp
from jax import lax

D = 512
MEDOIDS = 32768
TILE = 128
LMAX = 24
B_DEV = 16
GROUPS = 4
GROUP_SIZE = 8192
GROUP_TILES = 64
TILES = 64
FRAMES = 8192


def draw_tile_ids(key, part):
    group_tiles = MEDOIDS // (GROUPS * TILE)
    base = jax.random.fold_in(key, 11)
    keys = jax.random.split(base, GROUPS * TILES)
    lists = jax.vmap(lambda one: jax.random.permutation(one, group_tiles)[:LMAX])(keys)
    return lists.reshape(GROUPS, TILES, LMAX).astype(jnp.int32)


def draw_tile_counts(key, part):
    base = jax.random.fold_in(key, 23)
    first_key, second_key, third_key = jax.random.split(base, 3)
    members = TILES // B_DEV
    level = jax.random.randint(first_key, (members,), 0, 4)
    upper = LMAX // 8 * jnp.left_shift(jnp.ones_like(level), level)
    upper = jnp.repeat(upper, B_DEV)
    counts = jax.random.randint(second_key, (GROUPS, TILES), 1, upper[None, :] + 1)
    forced = jax.random.randint(third_key, (), 0, TILES)
    counts = counts.at[:, forced].set(LMAX)
    return counts.astype(jnp.int32)


def draw_plan(key, part):
    base = jax.random.fold_in(key, 37)
    first_key, second_key, third_key, fourth_key = jax.random.split(base, 4)
    members = TILES // B_DEV
    shuffled = jax.random.permutation(first_key, members)
    entries = jnp.arange(B_DEV)
    picks = entries % members
    shifts = shuffled[picks]
    relabel = jax.random.permutation(second_key, members)
    relabel_inverse = jnp.zeros((members,), jnp.int32).at[relabel].set(jnp.arange(members, dtype=jnp.int32))
    target_perm = jax.vmap(lambda one: jax.random.permutation(one, B_DEV))(jax.random.split(third_key, members))
    source_perm = jax.vmap(lambda one: jax.random.permutation(one, B_DEV))(jax.random.split(fourth_key, members))
    target = jnp.arange(members)[:, None]
    entry = entries[None, :]
    source = (relabel_inverse[target] - shifts[entry]) % members
    source_tile = source * B_DEV + source_perm[source, entry]
    position = target * B_DEV + target_perm[target, entry]
    plan = jnp.zeros((TILES,), jnp.int32).at[position.reshape(-1)].set(source_tile.reshape(-1).astype(jnp.int32))
    return plan


def levels(stream_key, shape, cuts, least, high):
    level, own = 1.0, jax.random.fold_in(stream_key, 6)
    for axis_at, shards_of in cuts:
        heights = jnp.exp(jax.random.uniform(jax.random.fold_in(own, axis_at), (shards_of,), jnp.float32, least / len(cuts), high / len(cuts)))
        level = level * jnp.repeat(heights, shape[axis_at] // shards_of).reshape([-1 if axis == axis_at else 1 for axis in range(len(shape))])
    return level


def scatter_about(rng, dims, deviation, limit, cuts=(), held_as=jnp.bfloat16):
    array = jax.random.normal(rng, dims, jnp.float32) * deviation
    if len(cuts) > 0:
        array = levels(rng, dims, cuts, -0.22, 0.18) * array
    return jnp.clip(array, min=-limit, max=limit).astype(held_as)


def setup_inputs(seed: int = 0, part: int = 0) -> dict:
    arg_keys = jax.random.split(jax.random.key(seed), 6)
    own_keys = jax.random.split(jax.random.fold_in(arg_keys[5], part), 6)
    return {
        "frames": scatter_about(own_keys[0], (FRAMES, D), 1.0, 6.0, ((0, 4),)),
        "medoids": scatter_about(arg_keys[1], (GROUPS, GROUP_SIZE, D), 1.0, 6.0, ((0, 4), (1, 4))),
        "tile_ids": draw_tile_ids(jax.random.fold_in(jax.random.fold_in(arg_keys[5], part), 71), part),
        "tile_counts": draw_tile_counts(jax.random.fold_in(jax.random.fold_in(arg_keys[5], part), 71), part),
        "plan": draw_plan(jax.random.fold_in(jax.random.fold_in(arg_keys[5], part), 71), part),
    }


big_value = 1e30
per_block = 8


def fold_two(left_one, left_two, right_one, right_two):
    first = jnp.minimum(left_one, right_one)
    second = jnp.minimum(jnp.maximum(left_one, right_one), jnp.minimum(left_two, right_two))
    return first, second


def tile_pass(frame_tile, ids, count, group_rows, group_norm):
    width = frame_tile.shape[1]
    rows_tile = frame_tile.shape[0]
    frame_norm = jnp.sum(jnp.square(frame_tile.astype(jnp.float32)), axis=1)

    def step(block, carry):
        start = (block * per_block).astype(jnp.int32)
        chosen = lax.dynamic_slice_in_dim(ids, start, per_block)
        live = (start + jnp.arange(per_block, dtype=jnp.int32)) < count
        rows = group_rows[chosen].reshape(per_block * rows_tile, width)
        norms = group_norm[chosen].reshape(per_block * rows_tile)
        inner = lax.dot_general(frame_tile, rows, (((1,), (1,)), ((), ())), preferred_element_type=jnp.float32)
        dist = (frame_norm[:, None] + norms[None, :] - 2.0 * inner) / width
        keep = jnp.repeat(live, rows_tile)
        dist = jnp.where(keep[None, :], dist, jnp.float32(big_value))
        lowest = -lax.top_k(-dist, 2)[0]
        return fold_two(carry[0], carry[1], lowest[:, 0], lowest[:, 1])

    start_pair = (jnp.full((rows_tile,), big_value, jnp.float32), jnp.full((rows_tile,), big_value, jnp.float32))
    blocks = (count + per_block - 1) // per_block
    return lax.fori_loop(0, blocks, step, start_pair)


def reference(frames, medoids, tile_ids, tile_counts, plan):
    tiles = frames.reshape(TILES, TILE, D)
    rows = medoids.reshape(GROUPS, GROUP_TILES, TILE, D)
    norms = jnp.sum(jnp.square(medoids.astype(jnp.float32)), axis=2).reshape(GROUPS, GROUP_TILES, TILE)

    def one_tile(index):
        best_one = jnp.full((TILE,), big_value, jnp.float32)
        best_two = jnp.full((TILE,), big_value, jnp.float32)
        for group in range(GROUPS):
            found_one, found_two = tile_pass(tiles[index], tile_ids[group, index], tile_counts[group, index], rows[group], norms[group])
            best_one, best_two = fold_two(best_one, best_two, found_one, found_two)
        return best_one, best_two

    first, second_all = lax.map(one_tile, jnp.arange(TILES, dtype=jnp.int32))
    return first[plan].reshape(FRAMES), second_all[plan].reshape(FRAMES)
```

```python
import functools

import jax
import jax.numpy as jnp
from jax import lax
from jax.experimental import pallas as pl
from jax.experimental.pallas import tpu as pltpu
from jax.sharding import PartitionSpec as P

TILE = 128


big_value = 1e30
per_block = 8
unroll = 4


def fold_two(left_one, left_two, right_one, right_two):
    first = jnp.minimum(left_one, right_one)
    second = jnp.minimum(jnp.maximum(left_one, right_one), jnp.minimum(left_two, right_two))
    return (first, second)


def tile_pass(frame_tile, ids, count, group_rows, group_norm):
    width = frame_tile.shape[1]
    rows_tile = frame_tile.shape[0]
    frame_norm = jnp.sum(jnp.square(frame_tile.astype(jnp.float32)), axis=1)

    def step(block, carry):
        start = (block * per_block).astype(jnp.int32)
        chosen = lax.dynamic_slice_in_dim(ids, start, per_block)
        live = start + jnp.arange(per_block, dtype=jnp.int32) < count
        rows = group_rows[chosen].reshape(per_block * rows_tile, width)
        norms = group_norm[chosen].reshape(per_block * rows_tile)
        inner = lax.dot_general(
            frame_tile, rows, (((1,), (1,)), ((), ())), preferred_element_type=jnp.float32
        )
        dist = (frame_norm[:, None] + norms[None, :] - 2.0 * inner) / width
        keep = jnp.repeat(live, rows_tile)
        dist = jnp.where(keep[None, :], dist, jnp.float32(big_value))
        lowest = -lax.top_k(-dist, 2)[0]
        return fold_two(carry[0], carry[1], lowest[:, 0], lowest[:, 1])

    start_pair = (
        jnp.full((rows_tile,), big_value, jnp.float32),
        jnp.full((rows_tile,), big_value, jnp.float32),
    )
    blocks = (count + per_block - 1) // per_block
    return lax.fori_loop(0, blocks, step, start_pair)


def all_tiles(tiles, ids, counts, group_rows, group_norm):
    number = tiles.shape[0]

    def one_tile(index, carry):
        found_one, found_two = tile_pass(
            tiles[index], ids[index], counts[index], group_rows, group_norm
        )
        return (carry[0].at[index].set(found_one), carry[1].at[index].set(found_two))

    empty = jnp.zeros((number, TILE), jnp.float32)
    return lax.fori_loop(0, number, one_tile, (empty, empty))


def across_groups(first, second):
    every_one, every_two = (
        lax.all_gather(first[None], "medoids", axis=0, tiled=True),
        lax.all_gather(second[None], "medoids", axis=0, tiled=True),
    )
    best_one, best_two = (every_one[0], every_two[0])
    for group in range(1, every_one.shape[0]):
        best_one, best_two = fold_two(best_one, best_two, every_one[group], every_two[group])
    return (best_one, best_two)


def gathered_medoids(frames, medoids, tile_ids, tile_counts, plan):
    width = frames.shape[1]
    blocks = frames.shape[0] // TILE
    members = lax.axis_size("frames")
    member = lax.axis_index("frames")
    capacity = (blocks + members - 1) // members
    group = lax.all_gather(medoids[0], "frames", axis=0, tiled=True)
    group_tiles = group.shape[0] // TILE
    group_rows = group.reshape(group_tiles, TILE, width)
    group_norm = jnp.sum(jnp.square(group.astype(jnp.float32)), axis=1).reshape(group_tiles, TILE)
    total = plan.shape[0]
    position = jnp.zeros((total,), jnp.int32).at[plan].set(jnp.arange(total, dtype=jnp.int32))
    target = (position // blocks).reshape(members, blocks)
    matching = target[:, :, None] == target[:, None, :]
    earlier = jnp.arange(blocks)[None, :] < jnp.arange(blocks)[:, None]
    slot_table = jnp.sum(jnp.logical_and(matching, earlier[None]), axis=2)
    my_target = lax.dynamic_index_in_dim(target, member, 0, keepdims=False)
    my_slot = lax.dynamic_index_in_dim(slot_table, member, 0, keepdims=False)
    arriving = lax.dynamic_slice_in_dim(plan, member * blocks, blocks)
    sender = arriving // blocks
    sender_slot = slot_table.reshape(-1)[arriving]
    tiles = frames.reshape(blocks, TILE, width)
    outgoing_tiles = (
        jnp.zeros((members, capacity, TILE, width), frames.dtype).at[my_target, my_slot].set(tiles)
    )
    outgoing_ids = (
        jnp.zeros((members, capacity, tile_ids.shape[2]), jnp.int32)
        .at[my_target, my_slot]
        .set(tile_ids[0])
    )
    outgoing_counts = (
        jnp.zeros((members, capacity), jnp.int32).at[my_target, my_slot].set(tile_counts[0])
    )
    incoming_tiles, incoming_ids, incoming_counts = (
        lax.all_to_all(outgoing_tiles, "frames", split_axis=0, concat_axis=0, tiled=True),
        lax.all_to_all(outgoing_ids, "frames", split_axis=0, concat_axis=0, tiled=True),
        lax.all_to_all(outgoing_counts, "frames", split_axis=0, concat_axis=0, tiled=True),
    )
    placed_tiles = incoming_tiles[sender, sender_slot]
    placed_ids = incoming_ids[sender, sender_slot]
    placed_counts = incoming_counts[sender, sender_slot]
    first, second = all_tiles(placed_tiles, placed_ids, placed_counts, group_rows, group_norm)
    first, second = across_groups(first, second)
    return (first.reshape(-1), second.reshape(-1))


def sublane_pair(one, two):
    rows = one.shape[0]
    while rows > 8:
        half = rows // 2
        one, two = fold_two(one[:half], two[:half], one[half:], two[half:])
        rows = half
    for shift in (4, 2, 1):
        one, two = fold_two(one, two, pltpu.roll(one, shift, 0), pltpu.roll(two, shift, 0))
    return one[0:1], two[0:1]


def search_kernel(
    groups,
    where_ref,
    lists_ref,
    own_frames,
    frames_1,
    frames_2,
    frames_3a,
    frames_3b,
    own_group,
    near_group,
    far_a,
    far_b,
    far_c,
    last_a,
    last_b,
    last_c,
    out_ref,
    rows_buf,
    frames_buf,
    norm_buf,
    entry_ref,
    number_ref,
    sems,
):
    tile_rows = own_group.shape[0]
    tiles_here = tile_rows // TILE
    quarter = frames_1.shape[0]
    quarter_tiles = quarter // TILE
    members = frames_buf.shape[0] // quarter
    width = rows_buf.shape[1]
    longest = lists_ref.shape[3] - 1
    member = where_ref[0]
    piece = where_ref[1]
    slab = where_ref[2]
    side = far_a.shape[0]
    middle = far_b.shape[0]
    near_side = slab * (tile_rows - side)
    other_side = (1 - slab) * (tile_rows - side)

    copies = []

    def bring(source, target, start, rows):
        copies.append(
            pltpu.make_async_copy(
                source, target.at[pl.ds(pl.multiple_of(start, TILE), rows)], sems.at[len(copies)]
            )
        )

    bring(own_group, rows_buf, 0, tile_rows)
    bring(near_group, rows_buf, tile_rows, tile_rows)
    for slot, (first_piece, second_piece, third_piece) in (
        (2, (far_a, far_b, far_c)),
        (3, (last_a, last_b, last_c)),
    ):
        bring(first_piece, rows_buf, slot * tile_rows + near_side, side)
        bring(second_piece, rows_buf, slot * tile_rows + side, middle)
        bring(third_piece, rows_buf, slot * tile_rows + other_side, side)
    bring(own_frames.at[pl.ds(pl.multiple_of(piece * quarter, TILE), quarter)], frames_buf, 0, quarter)
    bring(frames_1, frames_buf, quarter, quarter)
    bring(frames_2, frames_buf, 2 * quarter, quarter)
    for copy in copies:
        copy.start()
    inner_member = jnp.logical_and(member > 0, member < members - 1)
    last_sem = sems.at[len(copies)]
    last_target = frames_buf.at[pl.ds(3 * quarter, quarter)]

    @pl.when(inner_member)
    def _():
        pltpu.make_async_copy(frames_3a, last_target, last_sem).start()

    @pl.when(jnp.logical_not(inner_member))
    def _():
        pltpu.make_async_copy(frames_3b, last_target, last_sem).start()

    low = member * tiles_here

    def compact(tile, _):
        number = jnp.int32(0)
        for slot in range(groups):
            count = lists_ref[tile // quarter_tiles, slot, tile % quarter_tiles, longest]

            def take(at, number, slot=slot):
                entry = lists_ref[tile // quarter_tiles, slot, tile % quarter_tiles, at] - low
                entry_ref[tile, number] = entry + slot * tiles_here
                inside = jnp.logical_and(entry >= 0, entry < tiles_here)
                return number + inside.astype(jnp.int32)

            number = lax.fori_loop(0, count, take, number)
        number_ref[tile] = number
        return 0

    lax.fori_loop(0, members * quarter_tiles, compact, 0)

    for copy in copies:
        copy.wait()
    pltpu.make_async_copy(frames_3a, last_target, last_sem).wait()

    total_tiles = groups * tiles_here
    norm_buf[pl.ds(total_tiles * TILE, TILE), :] = jnp.full((TILE, TILE), big_value, jnp.float32)

    def norms(tile, _):
        start = pl.multiple_of(tile * TILE, TILE)
        rows = rows_buf[pl.ds(start, TILE), :].astype(jnp.float32)
        norm = 0.5 * jnp.sum(rows * rows, axis=1, keepdims=True)
        norm_buf[pl.ds(start, TILE), :] = jnp.broadcast_to(norm, (TILE, TILE))
        return 0

    lax.fori_loop(0, total_tiles, norms, 0)

    keep = 32

    def one_tile(tile, _):
        start = pl.multiple_of(tile * TILE, TILE)
        frame_tile = frames_buf[pl.ds(start, TILE), :]
        number = number_ref[tile]

        def block(at, carry):
            one, two = carry
            picked, picked_norm = [], []
            for step in range(unroll):
                place = at * unroll + step
                live = place < number
                entry = entry_ref[tile, place]
                row = pl.multiple_of(jnp.where(live, entry, 0) * TILE, TILE)
                picked.append(rows_buf[pl.ds(row, TILE), :])
                row = pl.multiple_of(jnp.where(live, entry, total_tiles) * TILE, TILE)
                picked_norm.append(norm_buf[pl.ds(row, TILE), :])
            inner = lax.dot_general(
                jnp.concatenate(picked, axis=0),
                frame_tile,
                (((1,), (1,)), ((), ())),
                preferred_element_type=jnp.float32,
            )
            dist = jnp.concatenate(picked_norm, axis=0) - inner
            for at_row in range(0, unroll * TILE, keep):
                part = dist[at_row : at_row + keep]
                two = jnp.minimum(two, jnp.maximum(one, part))
                one = jnp.minimum(one, part)
            return one, two

        empty = jnp.full((keep, TILE), big_value, jnp.float32)
        one, two = lax.fori_loop(0, (number + unroll - 1) // unroll, block, (empty, empty))
        one, two = sublane_pair(one, two)
        squares = frame_tile.astype(jnp.float32)
        squares = squares * squares
        total = squares[:, 0:TILE]
        for at_lane in range(TILE, width, TILE):
            total = total + squares[:, at_lane : at_lane + TILE]
        frame_norm = jnp.sum(total.T, axis=0, keepdims=True)
        block_of = jnp.bitwise_xor(member, tile // quarter_tiles)
        row = block_of * quarter_tiles + tile % quarter_tiles
        out_ref[0, pl.ds(row, 1), :] = (frame_norm + 2.0 * one) / width
        out_ref[1, pl.ds(row, 1), :] = (frame_norm + 2.0 * two) / width
        return 0

    lax.fori_loop(0, members * quarter_tiles, one_tile, 0)


def pick_kernel(where_ref, plan_ref, part_0, part_1, part_2, part_3, first_ref, second_ref, every):
    member = where_ref[0]
    piece = where_ref[1]
    blocks = first_ref.shape[0]
    parts = (part_0, part_1, part_2, part_3)
    quarter_tiles = blocks // len(parts)
    rows = part_0.shape[1]
    for slot, part in enumerate(parts):
        every[:, slot * rows : (slot + 1) * rows, :] = part[...]
    for place in range(blocks):
        tile = plan_ref[member * blocks + place]
        block_of = tile // blocks
        inside = tile - block_of * blocks
        part = inside // quarter_tiles
        row = jnp.bitwise_xor(part, piece) * rows + block_of * quarter_tiles + (inside - part * quarter_tiles)
        first_ref[pl.ds(place, 1), :] = every[0, pl.ds(row, 1), :]
        second_ref[pl.ds(place, 1), :] = every[1, pl.ds(row, 1), :]


def exchanged(number, distance):
    return [(at, at ^ distance) for at in range(number)]


def gathered_frames(frames, medoids, tile_ids, tile_counts, plan):
    width = frames.shape[1]
    blocks = frames.shape[0] // TILE
    members = lax.axis_size("frames")
    groups = lax.axis_size("medoids")
    member = lax.axis_index("frames")
    piece = lax.axis_index("medoids")
    slab = lax.axis_index("slab")
    rows = medoids[0]
    tile_rows = rows.shape[0]
    quarter_tiles = blocks // groups
    quarter = quarter_tiles * TILE
    side = tile_rows // TILE // 3 * TILE

    mine = lax.dynamic_slice_in_dim(frames, piece * quarter, quarter)
    frames_2 = lax.ppermute(mine, "frames", exchanged(members, 2))
    frames_1 = lax.ppermute(mine, "frames", exchanged(members, 1))
    frames_3a = lax.ppermute(mine, "frames", [(1, 2), (2, 1)])
    frames_3b = lax.ppermute(frames_2, "frames", [(2, 3), (1, 0)])

    edge = lax.dynamic_slice_in_dim(rows, slab * (tile_rows - side), side)
    far_a = lax.ppermute(edge, "medoids", exchanged(groups, 2))
    far_b = lax.ppermute(rows[side : tile_rows - side], "medoids", exchanged(groups, 2))
    far_c = lax.ppermute(far_a, "slab", exchanged(2, 1))
    near_group = lax.ppermute(rows, "medoids", exchanged(groups, 1))
    last_a = lax.ppermute(far_a, "medoids", exchanged(groups, 1))
    last_b = lax.ppermute(far_b, "medoids", exchanged(groups, 1))
    last_c = lax.ppermute(far_c, "medoids", exchanged(groups, 1))

    listed = jnp.concatenate([tile_ids[0], tile_counts[0][:, None]], axis=1)
    pair = jnp.stack([listed, lax.ppermute(listed, "medoids", exchanged(groups, 1))])
    lists = jnp.concatenate([pair, lax.ppermute(pair, "medoids", exchanged(groups, 2))], axis=0)
    lists = lax.dynamic_slice_in_dim(lists, piece * quarter_tiles, quarter_tiles, axis=1)
    lists = jnp.stack(
        [lists] + [lax.ppermute(lists, "frames", exchanged(members, at)) for at in (1, 2, 3)]
    )

    where = jnp.stack([member, piece, slab]).astype(jnp.int32)
    hbm = pl.BlockSpec(memory_space=pl.ANY)
    scalar = pl.BlockSpec(memory_space=pltpu.SMEM)
    vector = pl.BlockSpec(memory_space=pltpu.VMEM)
    total_rows = groups * tile_rows
    total_frames = members * quarter
    found = pl.pallas_call(
        functools.partial(search_kernel, groups),
        out_shape=jax.ShapeDtypeStruct((2, members * quarter_tiles, TILE), jnp.float32),
        in_specs=[scalar, scalar] + [hbm] * 13,
        out_specs=vector,
        scratch_shapes=[
            pltpu.VMEM((total_rows, width), jnp.bfloat16),
            pltpu.VMEM((total_frames, width), jnp.bfloat16),
            pltpu.VMEM((total_rows + TILE, TILE), jnp.float32),
            pltpu.SMEM((members * quarter_tiles, groups * tile_ids.shape[2] + 8), jnp.int32),
            pltpu.SMEM((members * quarter_tiles,), jnp.int32),
            pltpu.SemaphoreType.DMA((16,)),
        ],
        name="search",
    )(
        where, lists, frames, frames_1, frames_2, frames_3a, frames_3b,
        rows, near_group, far_a, far_b, far_c, last_a, last_b, last_c,
    )

    one, two = found[0], found[1]
    for at in (1, 2, 3):
        other = lax.ppermute(found, "frames", exchanged(members, at))
        one, two = fold_two(one, two, other[0], other[1])
    merged = jnp.stack([one, two])
    parts = [merged] + [lax.ppermute(merged, "medoids", exchanged(groups, at)) for at in (1, 2, 3)]
    first, second = pl.pallas_call(
        pick_kernel,
        out_shape=(jax.ShapeDtypeStruct((blocks, TILE), jnp.float32),) * 2,
        in_specs=[scalar, scalar] + [vector] * 4,
        out_specs=(vector, vector),
        scratch_shapes=[pltpu.VMEM((2, groups * members * quarter_tiles, TILE), jnp.float32)],
        name="pick",
    )(where, plan, *parts)
    return (first.reshape(-1), second.reshape(-1))


def solution(mesh):
    placed = (
        P(("slab", "frames"), None),
        P("medoids", "frames", None),
        P("medoids", ("slab", "frames"), None),
        P("medoids", ("slab", "frames")),
        P("slab"),
    )

    def per_device(frames, medoids, tile_ids, tile_counts, plan):
        blocks = frames.shape[0] // TILE
        quarters = mesh.shape["frames"] == 4 and mesh.shape["medoids"] == 4 and mesh.shape["slab"] == 2
        if quarters and blocks % 4 == 0 and medoids.shape[1] // TILE >= 3:
            return gathered_frames(frames, medoids, tile_ids, tile_counts, plan)
        return gathered_medoids(frames, medoids, tile_ids, tile_counts, plan)

    return jax.shard_map(
        per_device,
        mesh=mesh,
        in_specs=placed,
        out_specs=(P(("slab", "frames")), P(("slab", "frames"))),
        check_vma=False,
    )
```

```python
import functools

import jax
import jax.numpy as jnp
from jax import lax
from jax.experimental import pallas as pl
from jax.experimental.pallas import tpu as pltpu
from jax.sharding import PartitionSpec as P


TILE = 128


big_value = 1e30
per_block = 8
unroll = 4


def fold_two(left_one, left_two, right_one, right_two):
    first = jnp.minimum(left_one, right_one)
    second = jnp.minimum(jnp.maximum(left_one, right_one), jnp.minimum(left_two, right_two))
    return (first, second)


def tile_pass(frame_tile, ids, count, group_rows, group_norm):
    width = frame_tile.shape[1]
    rows_tile = frame_tile.shape[0]
    frame_norm = jnp.sum(jnp.square(frame_tile.astype(jnp.float32)), axis=1)

    def step(block, carry):
        start = (block * per_block).astype(jnp.int32)
        chosen = lax.dynamic_slice_in_dim(ids, start, per_block)
        live = start + jnp.arange(per_block, dtype=jnp.int32) < count
        rows = group_rows[chosen].reshape(per_block * rows_tile, width)
        norms = group_norm[chosen].reshape(per_block * rows_tile)
        inner = lax.dot_general(
            frame_tile, rows, (((1,), (1,)), ((), ())), preferred_element_type=jnp.float32
        )
        dist = (frame_norm[:, None] + norms[None, :] - 2.0 * inner) / width
        keep = jnp.repeat(live, rows_tile)
        dist = jnp.where(keep[None, :], dist, jnp.float32(big_value))
        lowest = -lax.top_k(-dist, 2)[0]
        return fold_two(carry[0], carry[1], lowest[:, 0], lowest[:, 1])

    start_pair = (
        jnp.full((rows_tile,), big_value, jnp.float32),
        jnp.full((rows_tile,), big_value, jnp.float32),
    )
    blocks = (count + per_block - 1) // per_block
    return lax.fori_loop(0, blocks, step, start_pair)


def all_tiles(tiles, ids, counts, group_rows, group_norm):
    number = tiles.shape[0]

    def one_tile(index, carry):
        found_one, found_two = tile_pass(
            tiles[index], ids[index], counts[index], group_rows, group_norm
        )
        return (carry[0].at[index].set(found_one), carry[1].at[index].set(found_two))

    empty = jnp.zeros((number, TILE), jnp.float32)
    return lax.fori_loop(0, number, one_tile, (empty, empty))


def across_groups(first, second):
    every_one, every_two = (
        lax.all_gather(first[None], "medoids", axis=0, tiled=True),
        lax.all_gather(second[None], "medoids", axis=0, tiled=True),
    )
    best_one, best_two = (every_one[0], every_two[0])
    for group in range(1, every_one.shape[0]):
        best_one, best_two = fold_two(best_one, best_two, every_one[group], every_two[group])
    return (best_one, best_two)


def gathered_medoids(frames, medoids, tile_ids, tile_counts, plan):
    width = frames.shape[1]
    blocks = frames.shape[0] // TILE
    members = lax.axis_size("frames")
    member = lax.axis_index("frames")
    capacity = (blocks + members - 1) // members
    group = lax.all_gather(medoids[0], "frames", axis=0, tiled=True)
    group_tiles = group.shape[0] // TILE
    group_rows = group.reshape(group_tiles, TILE, width)
    group_norm = jnp.sum(jnp.square(group.astype(jnp.float32)), axis=1).reshape(group_tiles, TILE)
    total = plan.shape[0]
    position = jnp.zeros((total,), jnp.int32).at[plan].set(jnp.arange(total, dtype=jnp.int32))
    target = (position // blocks).reshape(members, blocks)
    matching = target[:, :, None] == target[:, None, :]
    earlier = jnp.arange(blocks)[None, :] < jnp.arange(blocks)[:, None]
    slot_table = jnp.sum(jnp.logical_and(matching, earlier[None]), axis=2)
    my_target = lax.dynamic_index_in_dim(target, member, 0, keepdims=False)
    my_slot = lax.dynamic_index_in_dim(slot_table, member, 0, keepdims=False)
    arriving = lax.dynamic_slice_in_dim(plan, member * blocks, blocks)
    sender = arriving // blocks
    sender_slot = slot_table.reshape(-1)[arriving]
    tiles = frames.reshape(blocks, TILE, width)
    outgoing_tiles = (
        jnp.zeros((members, capacity, TILE, width), frames.dtype).at[my_target, my_slot].set(tiles)
    )
    outgoing_ids = (
        jnp.zeros((members, capacity, tile_ids.shape[2]), jnp.int32)
        .at[my_target, my_slot]
        .set(tile_ids[0])
    )
    outgoing_counts = (
        jnp.zeros((members, capacity), jnp.int32).at[my_target, my_slot].set(tile_counts[0])
    )
    incoming_tiles, incoming_ids, incoming_counts = (
        lax.all_to_all(outgoing_tiles, "frames", split_axis=0, concat_axis=0, tiled=True),
        lax.all_to_all(outgoing_ids, "frames", split_axis=0, concat_axis=0, tiled=True),
        lax.all_to_all(outgoing_counts, "frames", split_axis=0, concat_axis=0, tiled=True),
    )
    placed_tiles = incoming_tiles[sender, sender_slot]
    placed_ids = incoming_ids[sender, sender_slot]
    placed_counts = incoming_counts[sender, sender_slot]
    first, second = all_tiles(placed_tiles, placed_ids, placed_counts, group_rows, group_norm)
    first, second = across_groups(first, second)
    return (first.reshape(-1), second.reshape(-1))


def column_of(squares):
    total = squares[:, 0:TILE]
    for at_lane in range(TILE, squares.shape[1], TILE):
        total = total + squares[:, at_lane : at_lane + TILE]
    return jnp.sum(total.T, axis=0, keepdims=True)


def row_pair(one, two):
    one, two = one.T, two.T
    rows = one.shape[0]
    while rows > 8:
        half = rows // 2
        one, two = fold_two(one[:half], two[:half], one[half:], two[half:])
        rows = half
    for shift in (4, 2, 1):
        one, two = fold_two(one, two, pltpu.roll(one, shift, 0), pltpu.roll(two, shift, 0))
    return one[0:1], two[0:1]


def prepare_kernel(members, where_ref, ids_ref, counts_ref, group_ref, lists_ref, norms_ref):
    tiles_here = group_ref.shape[0] // TILE
    lanes = lists_ref.shape[1] // members
    member = where_ref[0]

    def split(tile, _):
        def take(at, numbers):
            entry = ids_ref[tile, at]
            owner = entry // tiles_here
            distance = jnp.bitwise_xor(owner, member)
            place = jnp.int32(0)
            for shard in range(members):
                place = jnp.where(distance == shard, numbers[shard], place)
            lists_ref[tile, distance * lanes + place] = entry - owner * tiles_here
            return tuple(
                numbers[shard] + (distance == shard).astype(jnp.int32) for shard in range(members)
            )

        numbers = lax.fori_loop(0, counts_ref[0, tile], take, (jnp.int32(0),) * members)
        for shard in range(members):
            lists_ref[tile, shard * lanes + lanes - 1] = numbers[shard]
        return 0

    lax.fori_loop(0, ids_ref.shape[0], split, 0)

    for tile in range(tiles_here):
        rows = group_ref[tile * TILE : (tile + 1) * TILE, :].astype(jnp.float32)
        norms_ref[tile : tile + 1, :] = 0.5 * column_of(rows * rows)


def search_tile(frame_tile, slots, zslot, tile, lists_ref, rows_ref, norms_ref, dummy, base):
    last_lane = lists_ref.shape[3] - 1
    tiles_here = base
    ends = []
    number = jnp.int32(0)
    for slot in slots:
        number = number + lists_ref[zslot, slot, tile, last_lane]
        ends.append(number)

    def block(at, carry):
        one, two = carry
        picked, picked_norm = [], []
        for step in range(unroll):
            place = at * unroll + step
            live = place < number
            slot = jnp.int32(slots[0])
            start = jnp.int32(0)
            for index in range(1, len(slots)):
                beyond = place >= ends[index - 1]
                slot = jnp.where(beyond, slots[index], slot)
                start = jnp.where(beyond, ends[index - 1], start)
            place = jnp.where(live, place - start, 0)
            entry = lists_ref[zslot, slot, tile, place] + (slot - slots[0]) * tiles_here
            entry = jnp.where(live, entry, 0)
            picked.append(rows_ref[pl.ds(pl.multiple_of(entry * TILE, TILE), TILE), :])
            picked_norm.append(norms_ref[pl.ds(jnp.where(live, entry, dummy), 1), :])
        inner = lax.dot_general(
            frame_tile,
            jnp.concatenate(picked, axis=0),
            (((1,), (1,)), ((), ())),
            preferred_element_type=jnp.float32,
        )
        for step in range(unroll):
            part = picked_norm[step] - inner[:, step * TILE : (step + 1) * TILE]
            two = jnp.minimum(two, jnp.maximum(one, part))
            one = jnp.minimum(one, part)
        return one, two

    empty = jnp.full((TILE, TILE), big_value, jnp.float32)
    return lax.fori_loop(0, (number + unroll - 1) // unroll, block, (empty, empty))


def near_kernel(
    lists_ref, norms_in, own_group, near_group, own_frames, frames_1, frames_2,
    out_ref, rows_buf, frames_buf, norms_buf, sems,
):
    tile_rows = own_group.shape[0]
    tiles_here = tile_rows // TILE
    quarter = own_frames.shape[0]
    quarter_tiles = quarter // TILE
    copies = [
        pltpu.make_async_copy(own_group, rows_buf.at[pl.ds(0, tile_rows)], sems.at[0]),
        pltpu.make_async_copy(near_group, rows_buf.at[pl.ds(tile_rows, tile_rows)], sems.at[1]),
    ]
    for index, ref in enumerate((own_frames, frames_1, frames_2)):
        copies.append(
            pltpu.make_async_copy(
                ref, frames_buf.at[pl.ds(index * quarter, quarter)], sems.at[2 + index]
            )
        )
    for copy in copies:
        copy.start()
    dummy = 2 * tiles_here
    norms_buf[pl.ds(0, tiles_here), :] = norms_in[0]
    norms_buf[pl.ds(tiles_here, tiles_here), :] = norms_in[1]
    norms_buf[pl.ds(dummy, 1), :] = jnp.full((1, TILE), big_value, jnp.float32)
    out_ref[...] = jnp.full(out_ref.shape, big_value, jnp.float32)
    for copy in copies:
        copy.wait()

    def one_tile(index, _):
        zslot = index // quarter_tiles
        tile = index - zslot * quarter_tiles
        frame_tile = frames_buf[pl.ds(pl.multiple_of(index * TILE, TILE), TILE), :]
        one, two = search_tile(
            frame_tile, (0, 1), zslot, tile, lists_ref, rows_buf, norms_buf, dummy, tiles_here
        )
        one, two = row_pair(one, two)
        squares = frame_tile.astype(jnp.float32)
        out_ref[0, pl.ds(index, 1), :] = one
        out_ref[1, pl.ds(index, 1), :] = two
        out_ref[2, pl.ds(index, 1), :] = column_of(squares * squares)
        return 0

    lax.fori_loop(0, 3 * quarter_tiles, one_tile, 0)


def far_kernel(
    where_ref, lists_ref, norms_in, before_ref, own_group, near_group, far_a, far_b, far_c,
    last_a, last_b, last_c, own_frames, frames_1, frames_2, frames_3a, frames_3b,
    out_ref, rows_buf, frames_buf, norms_buf, found_buf, sems,
):
    tile_rows = own_group.shape[0]
    tiles_here = tile_rows // TILE
    groups = norms_in.shape[0]
    quarter = own_frames.shape[0]
    quarter_tiles = quarter // TILE
    width = own_frames.shape[1]
    members = frames_buf.shape[0] // quarter
    member = where_ref[0]
    slab = where_ref[2]
    side = far_a.shape[0]
    middle = far_b.shape[0]
    near_side = slab * (tile_rows - side)
    other_side = (1 - slab) * (tile_rows - side)

    copies = []

    def bring(source, target, start, rows):
        copies.append(
            pltpu.make_async_copy(
                source, target.at[pl.ds(pl.multiple_of(start, TILE), rows)], sems.at[len(copies)]
            )
        )

    for slot, (first_piece, second_piece, third_piece) in (
        (2, (far_a, far_b, far_c)),
        (3, (last_a, last_b, last_c)),
    ):
        bring(first_piece, rows_buf, slot * tile_rows + near_side, side)
        bring(second_piece, rows_buf, slot * tile_rows + side, middle)
        bring(third_piece, rows_buf, slot * tile_rows + other_side, side)
    bring(own_frames, frames_buf, 0, quarter)
    bring(frames_1, frames_buf, quarter, quarter)
    bring(frames_2, frames_buf, 2 * quarter, quarter)
    early = len(copies)
    bring(own_group, rows_buf, 0, tile_rows)
    bring(near_group, rows_buf, tile_rows, tile_rows)
    for copy in copies[:early]:
        copy.start()
    inner_member = jnp.logical_and(member > 0, member < members - 1)
    last_sem = sems.at[len(copies)]
    last_target = frames_buf.at[pl.ds(3 * quarter, quarter)]

    @pl.when(inner_member)
    def _():
        pltpu.make_async_copy(frames_3a, last_target, last_sem).start()

    @pl.when(jnp.logical_not(inner_member))
    def _():
        pltpu.make_async_copy(frames_3b, last_target, last_sem).start()

    for copy in copies[early:]:
        copy.start()

    dummy = groups * tiles_here
    for slot in range(groups):
        norms_buf[pl.ds(slot * tiles_here, tiles_here), :] = norms_in[slot]
    norms_buf[pl.ds(dummy, 1), :] = jnp.full((1, TILE), big_value, jnp.float32)
    found_buf[...] = before_ref[...]
    for copy in copies[:early]:
        copy.wait()

    far_rows = rows_buf.at[pl.ds(2 * tile_rows, 2 * tile_rows)]
    far_norms = norms_buf.at[pl.ds(2 * tiles_here, 2 * tiles_here + 8)]

    def one_tile(index, _):
        zslot = index // quarter_tiles
        tile = index - zslot * quarter_tiles
        frame_tile = frames_buf[pl.ds(pl.multiple_of(index * TILE, TILE), TILE), :]
        one, two = search_tile(
            frame_tile, (2, 3), zslot, tile, lists_ref, far_rows, far_norms, 2 * tiles_here, tiles_here
        )
        one, two = row_pair(one, two)
        one, two = fold_two(
            one, two, found_buf[0, pl.ds(index, 1), :], found_buf[1, pl.ds(index, 1), :]
        )
        found_buf[0, pl.ds(index, 1), :] = one
        found_buf[1, pl.ds(index, 1), :] = two
        return 0

    lax.fori_loop(0, 3 * quarter_tiles, one_tile, 0)
    pltpu.make_async_copy(frames_3a, last_target, last_sem).wait()
    for copy in copies[early:]:
        copy.wait()

    def last_tile(tile, _):
        index = 3 * quarter_tiles + tile
        frame_tile = frames_buf[pl.ds(pl.multiple_of(index * TILE, TILE), TILE), :]
        one, two = search_tile(
            frame_tile, tuple(range(groups)), 3, tile, lists_ref, rows_buf, norms_buf, dummy, tiles_here
        )
        one, two = row_pair(one, two)
        squares = frame_tile.astype(jnp.float32)
        found_buf[0, pl.ds(index, 1), :] = one
        found_buf[1, pl.ds(index, 1), :] = two
        found_buf[2, pl.ds(index, 1), :] = column_of(squares * squares)
        return 0

    lax.fori_loop(0, quarter_tiles, last_tile, 0)
    norm = found_buf[2]
    found_buf[0] = (norm + 2.0 * found_buf[0]) / width
    found_buf[1] = (norm + 2.0 * found_buf[1]) / width
    for index in range(members * quarter_tiles):
        block_of = jnp.bitwise_xor(member, index // quarter_tiles)
        row = block_of * quarter_tiles + index % quarter_tiles
        out_ref[0, pl.ds(row, 1), :] = found_buf[0, index : index + 1, :]
        out_ref[1, pl.ds(row, 1), :] = found_buf[1, index : index + 1, :]


def pick_kernel(where_ref, plan_ref, part_0, part_1, part_2, part_3, first_ref, second_ref, every):
    member = where_ref[0]
    piece = where_ref[1]
    blocks = first_ref.shape[0]
    parts = (part_0, part_1, part_2, part_3)
    quarter_tiles = blocks // len(parts)
    rows = part_0.shape[1]
    for slot, part in enumerate(parts):
        every[:, slot * rows : (slot + 1) * rows, :] = part[...]
    for place in range(blocks):
        tile = plan_ref[member * blocks + place]
        block_of = tile // blocks
        inside = tile - block_of * blocks
        part = inside // quarter_tiles
        row = jnp.bitwise_xor(part, piece) * rows + block_of * quarter_tiles + (inside - part * quarter_tiles)
        first_ref[pl.ds(place, 1), :] = every[0, pl.ds(row, 1), :]
        second_ref[pl.ds(place, 1), :] = every[1, pl.ds(row, 1), :]


def exchanged(number, distance):
    return [(at, at ^ distance) for at in range(number)]


def gathered_frames(frames, medoids, tile_ids, tile_counts, plan):
    width = frames.shape[1]
    blocks = frames.shape[0] // TILE
    members = lax.axis_size("frames")
    groups = lax.axis_size("medoids")
    member = lax.axis_index("frames")
    piece = lax.axis_index("medoids")
    slab = lax.axis_index("slab")
    rows = medoids[0]
    tile_rows = rows.shape[0]
    quarter_tiles = blocks // groups
    quarter = quarter_tiles * TILE
    side = tile_rows // TILE // 3 * TILE

    mine = lax.dynamic_slice_in_dim(frames, piece * quarter, quarter)
    frames_2 = lax.ppermute(mine, "frames", exchanged(members, 2))
    frames_1 = lax.ppermute(mine, "frames", exchanged(members, 1))
    frames_3a = lax.ppermute(mine, "frames", [(1, 2), (2, 1)])
    frames_3b = lax.ppermute(frames_2, "frames", [(2, 3), (1, 0)])

    edge = lax.dynamic_slice_in_dim(rows, slab * (tile_rows - side), side)
    far_a = lax.ppermute(edge, "medoids", exchanged(groups, 2))
    far_b = lax.ppermute(rows[side : tile_rows - side], "medoids", exchanged(groups, 2))
    far_c = lax.ppermute(far_a, "slab", exchanged(2, 1))
    near_group = lax.ppermute(rows, "medoids", exchanged(groups, 1))
    last_a = lax.ppermute(far_a, "medoids", exchanged(groups, 1))
    last_b = lax.ppermute(far_b, "medoids", exchanged(groups, 1))
    last_c = lax.ppermute(far_c, "medoids", exchanged(groups, 1))

    where = jnp.stack([member, piece, slab]).astype(jnp.int32)
    hbm = pl.BlockSpec(memory_space=pl.ANY)
    scalar = pl.BlockSpec(memory_space=pltpu.SMEM)
    vector = pl.BlockSpec(memory_space=pltpu.VMEM)
    tiles_here = tile_rows // TILE
    lanes = TILE // members
    listed, norms = pl.pallas_call(
        functools.partial(prepare_kernel, members),
        out_shape=(
            jax.ShapeDtypeStruct((blocks, members * lanes), jnp.int32),
            jax.ShapeDtypeStruct((tiles_here, TILE), jnp.float32),
        ),
        in_specs=[scalar, scalar, scalar, vector],
        out_specs=(scalar, vector),
        name="prepare",
    )(where, tile_ids[0], tile_counts, rows)
    packed = jnp.concatenate([listed.astype(jnp.float32), norms], axis=0)
    pair = jnp.stack([packed, lax.ppermute(packed, "medoids", exchanged(groups, 1))])
    far_pair = lax.ppermute(pair, "medoids", exchanged(groups, 2))
    packed = jnp.concatenate([pair, far_pair], axis=0)
    norms = packed[:, blocks:]
    lists = lax.dynamic_slice_in_dim(packed, piece * quarter_tiles, quarter_tiles, axis=1)
    lists = lists.astype(jnp.int32).reshape(groups, quarter_tiles, members, lanes)
    lists = jnp.stack(
        [lists[:, :, 0]]
        + [lax.ppermute(lists[:, :, at], "frames", exchanged(members, at)) for at in (1, 2, 3)]
    )

    total_tiles = members * quarter_tiles
    before = pl.pallas_call(
        near_kernel,
        out_shape=jax.ShapeDtypeStruct((3, total_tiles, TILE), jnp.float32),
        in_specs=[scalar, vector] + [hbm] * 5,
        out_specs=vector,
        scratch_shapes=[
            pltpu.VMEM((2 * tile_rows, width), jnp.bfloat16),
            pltpu.VMEM((3 * quarter, width), jnp.bfloat16),
            pltpu.VMEM((2 * tiles_here + 8, TILE), jnp.float32),
            pltpu.SemaphoreType.DMA((5,)),
        ],
        name="near_search",
    )(lists, norms, rows, near_group, mine, frames_1, frames_2)
    found = pl.pallas_call(
        far_kernel,
        out_shape=jax.ShapeDtypeStruct((2, total_tiles, TILE), jnp.float32),
        in_specs=[scalar, scalar, vector, vector] + [hbm] * 13,
        out_specs=vector,
        scratch_shapes=[
            pltpu.VMEM((groups * tile_rows, width), jnp.bfloat16),
            pltpu.VMEM((members * quarter, width), jnp.bfloat16),
            pltpu.VMEM((groups * tiles_here + 8, TILE), jnp.float32),
            pltpu.VMEM((3, total_tiles, TILE), jnp.float32),
            pltpu.SemaphoreType.DMA((16,)),
        ],
        name="far_search",
    )(
        where, lists, norms, before, rows, near_group, far_a, far_b, far_c, last_a, last_b, last_c,
        mine, frames_1, frames_2, frames_3a, frames_3b,
    )

    one, two = found[0], found[1]
    for at in (1, 2, 3):
        other = lax.ppermute(found, "frames", exchanged(members, at))
        one, two = fold_two(one, two, other[0], other[1])
    merged = jnp.stack([one, two])
    parts = [merged] + [lax.ppermute(merged, "medoids", exchanged(groups, at)) for at in (1, 2, 3)]
    first, second = pl.pallas_call(
        pick_kernel,
        out_shape=(jax.ShapeDtypeStruct((blocks, TILE), jnp.float32),) * 2,
        in_specs=[scalar, scalar] + [vector] * 4,
        out_specs=(vector, vector),
        scratch_shapes=[pltpu.VMEM((2, groups * members * quarter_tiles, TILE), jnp.float32)],
        name="pick",
    )(where, plan, *parts)
    return (first.reshape(-1), second.reshape(-1))


def solution(mesh):
    placed = (
        P(("slab", "frames"), None),
        P("medoids", "frames", None),
        P("medoids", ("slab", "frames"), None),
        P("medoids", ("slab", "frames")),
        P("slab"),
    )

    def per_device(frames, medoids, tile_ids, tile_counts, plan):
        blocks = frames.shape[0] // TILE
        quarters = mesh.shape["frames"] == 4 and mesh.shape["medoids"] == 4 and mesh.shape["slab"] == 2
        if quarters and blocks % 4 == 0 and medoids.shape[1] // TILE >= 3:
            return gathered_frames(frames, medoids, tile_ids, tile_counts, plan)
        return gathered_medoids(frames, medoids, tile_ids, tile_counts, plan)

    return jax.shard_map(
        per_device,
        mesh=mesh,
        in_specs=placed,
        out_specs=(P(("slab", "frames")), P(("slab", "frames"))),
        check_vma=False,
    )
```

```python
import functools

import jax
import jax.numpy as jnp
from jax import lax
from jax.experimental import pallas as pl
from jax.experimental.pallas import tpu as pltpu
from jax.sharding import PartitionSpec as P


TILE = 128


big_value = 1e30
per_block = 8
unroll = 4
together = 2
small_vmem = 8 << 20
large_vmem = 24 << 20


def fold_two(left_one, left_two, right_one, right_two):
    first = jnp.minimum(left_one, right_one)
    second = jnp.minimum(jnp.maximum(left_one, right_one), jnp.minimum(left_two, right_two))
    return (first, second)


def tile_pass(frame_tile, ids, count, group_rows, group_norm):
    width = frame_tile.shape[1]
    rows_tile = frame_tile.shape[0]
    frame_norm = jnp.sum(jnp.square(frame_tile.astype(jnp.float32)), axis=1)

    def step(block, carry):
        start = (block * per_block).astype(jnp.int32)
        chosen = lax.dynamic_slice_in_dim(ids, start, per_block)
        live = start + jnp.arange(per_block, dtype=jnp.int32) < count
        rows = group_rows[chosen].reshape(per_block * rows_tile, width)
        norms = group_norm[chosen].reshape(per_block * rows_tile)
        inner = lax.dot_general(
            frame_tile, rows, (((1,), (1,)), ((), ())), preferred_element_type=jnp.float32
        )
        dist = (frame_norm[:, None] + norms[None, :] - 2.0 * inner) / width
        keep = jnp.repeat(live, rows_tile)
        dist = jnp.where(keep[None, :], dist, jnp.float32(big_value))
        lowest = -lax.top_k(-dist, 2)[0]
        return fold_two(carry[0], carry[1], lowest[:, 0], lowest[:, 1])

    start_pair = (
        jnp.full((rows_tile,), big_value, jnp.float32),
        jnp.full((rows_tile,), big_value, jnp.float32),
    )
    blocks = (count + per_block - 1) // per_block
    return lax.fori_loop(0, blocks, step, start_pair)


def all_tiles(tiles, ids, counts, group_rows, group_norm):
    number = tiles.shape[0]

    def one_tile(index, carry):
        found_one, found_two = tile_pass(
            tiles[index], ids[index], counts[index], group_rows, group_norm
        )
        return (carry[0].at[index].set(found_one), carry[1].at[index].set(found_two))

    empty = jnp.zeros((number, TILE), jnp.float32)
    return lax.fori_loop(0, number, one_tile, (empty, empty))


def across_groups(first, second):
    every_one, every_two = (
        lax.all_gather(first[None], "medoids", axis=0, tiled=True),
        lax.all_gather(second[None], "medoids", axis=0, tiled=True),
    )
    best_one, best_two = (every_one[0], every_two[0])
    for group in range(1, every_one.shape[0]):
        best_one, best_two = fold_two(best_one, best_two, every_one[group], every_two[group])
    return (best_one, best_two)


def gathered_medoids(frames, medoids, tile_ids, tile_counts, plan):
    width = frames.shape[1]
    blocks = frames.shape[0] // TILE
    members = lax.axis_size("frames")
    member = lax.axis_index("frames")
    capacity = (blocks + members - 1) // members
    group = lax.all_gather(medoids[0], "frames", axis=0, tiled=True)
    group_tiles = group.shape[0] // TILE
    group_rows = group.reshape(group_tiles, TILE, width)
    group_norm = jnp.sum(jnp.square(group.astype(jnp.float32)), axis=1).reshape(group_tiles, TILE)
    total = plan.shape[0]
    position = jnp.zeros((total,), jnp.int32).at[plan].set(jnp.arange(total, dtype=jnp.int32))
    target = (position // blocks).reshape(members, blocks)
    matching = target[:, :, None] == target[:, None, :]
    earlier = jnp.arange(blocks)[None, :] < jnp.arange(blocks)[:, None]
    slot_table = jnp.sum(jnp.logical_and(matching, earlier[None]), axis=2)
    my_target = lax.dynamic_index_in_dim(target, member, 0, keepdims=False)
    my_slot = lax.dynamic_index_in_dim(slot_table, member, 0, keepdims=False)
    arriving = lax.dynamic_slice_in_dim(plan, member * blocks, blocks)
    sender = arriving // blocks
    sender_slot = slot_table.reshape(-1)[arriving]
    tiles = frames.reshape(blocks, TILE, width)
    outgoing_tiles = (
        jnp.zeros((members, capacity, TILE, width), frames.dtype).at[my_target, my_slot].set(tiles)
    )
    outgoing_ids = (
        jnp.zeros((members, capacity, tile_ids.shape[2]), jnp.int32)
        .at[my_target, my_slot]
        .set(tile_ids[0])
    )
    outgoing_counts = (
        jnp.zeros((members, capacity), jnp.int32).at[my_target, my_slot].set(tile_counts[0])
    )
    incoming_tiles, incoming_ids, incoming_counts = (
        lax.all_to_all(outgoing_tiles, "frames", split_axis=0, concat_axis=0, tiled=True),
        lax.all_to_all(outgoing_ids, "frames", split_axis=0, concat_axis=0, tiled=True),
        lax.all_to_all(outgoing_counts, "frames", split_axis=0, concat_axis=0, tiled=True),
    )
    placed_tiles = incoming_tiles[sender, sender_slot]
    placed_ids = incoming_ids[sender, sender_slot]
    placed_counts = incoming_counts[sender, sender_slot]
    first, second = all_tiles(placed_tiles, placed_ids, placed_counts, group_rows, group_norm)
    first, second = across_groups(first, second)
    return (first.reshape(-1), second.reshape(-1))


def column_of(squares):
    total = squares[:, 0:TILE]
    for at_lane in range(TILE, squares.shape[1], TILE):
        total = total + squares[:, at_lane : at_lane + TILE]
    return jnp.sum(total.T, axis=0, keepdims=True)


def row_pair(one, two):
    one, two = one.T, two.T
    rows = one.shape[0]
    while rows > 8:
        half = rows // 2
        one, two = fold_two(one[:half], two[:half], one[half:], two[half:])
        rows = half
    for shift in (4, 2, 1):
        one, two = fold_two(one, two, pltpu.roll(one, shift, 0), pltpu.roll(two, shift, 0))
    return one[0:1], two[0:1]


def split_kernel(members, where_ref, ids_ref, counts_ref, lists_ref):
    tiles_here = where_ref[3]
    lanes = lists_ref.shape[1] // members
    member = where_ref[0]

    def split(tile, _):
        for shard in range(members):
            lists_ref[tile, shard * lanes + lanes - 1] = 0

        def take(at, _):
            entry = ids_ref[tile, at]
            owner = jnp.int32(0)
            for shard in range(1, members):
                owner = owner + (entry >= shard * tiles_here).astype(jnp.int32)
            start = jnp.bitwise_xor(owner, member) * lanes
            place = lists_ref[tile, start + lanes - 1]
            lists_ref[tile, start + place] = entry - owner * tiles_here
            lists_ref[tile, start + lanes - 1] = place + 1
            return 0

        return lax.fori_loop(0, counts_ref[0, tile], take, 0)

    lax.fori_loop(0, ids_ref.shape[0], split, 0)


def norms_kernel(scale, *refs):
    norms_ref = refs[-1]
    row = 0
    for ref in refs[:-1]:
        for tile in range(ref.shape[0] // TILE):
            rows = ref[tile * TILE : (tile + 1) * TILE, :].astype(jnp.float32)
            norms_ref[row : row + 1, :] = scale * column_of(rows * rows)
            row += 1


def search(
    tiles, slots, first_tile, quarter_tiles, tiles_here, lists_ref, rows_ref, norms_ref,
    frames_ref, one_ref, two_ref, table_ref,
):
    last_lane = lists_ref.shape[3] - 1
    dummy = len(slots) * tiles_here
    shift = 16

    def place_of(index):
        zslot = index // quarter_tiles
        return zslot, index - zslot * quarter_tiles

    def ends_of(index):
        zslot, tile = place_of(index)
        ends, number = [], jnp.int32(0)
        for slot in slots:
            number = number + lists_ref[zslot, slot, tile, last_lane]
            ends.append(number)
        return ends

    def blocks_of(at, written):
        blocks = (ends_of(first_tile + at)[-1] + unroll - 1) // unroll

        def put(block, _):
            table_ref[written + block] = (block << shift) + at
            return 0

        lax.fori_loop(0, blocks, put, 0)
        return written + blocks

    written = lax.fori_loop(0, tiles, blocks_of, jnp.int32(0))
    for extra in range(together - 1):
        table_ref[written + extra] = jnp.int32(1 << (shift + 8))
    size = tiles * TILE
    one_ref[0:size, :] = jnp.full((size, TILE), big_value, jnp.float32)
    two_ref[0:size, :] = jnp.full((size, TILE), big_value, jnp.float32)

    def step(at_step, _):
        results = []
        for member in range(together):
            code = table_ref[at_step * together + member]
            at = jnp.bitwise_and(code, (1 << shift) - 1)
            block = code >> shift
            index = first_tile + at
            zslot, tile = place_of(index)
            ends = ends_of(index)
            picked, picked_norm = [], []
            for lane in range(unroll):
                place = block * unroll + lane
                live = place < ends[-1]
                slot, start = jnp.int32(0), jnp.int32(0)
                for number in range(1, len(slots)):
                    beyond = place >= ends[number - 1]
                    slot = jnp.where(beyond, number, slot)
                    start = jnp.where(beyond, ends[number - 1], start)
                place = jnp.where(live, place - start, 0)
                entry = lists_ref[zslot, slots[0] + slot, tile, place] + slot * tiles_here
                row = jnp.where(live, entry, 0) * TILE
                picked.append(rows_ref[pl.ds(pl.multiple_of(row, TILE), TILE), :])
                picked_norm.append(norms_ref[pl.ds(jnp.where(live, entry, dummy), 1), :])
            inner = lax.dot_general(
                frames_ref[pl.ds(pl.multiple_of(index * TILE, TILE), TILE), :],
                jnp.concatenate(picked, axis=0),
                (((1,), (1,)), ((), ())),
                preferred_element_type=jnp.float32,
            )
            results.append((at, picked_norm, inner))
        for at, picked_norm, inner in results:
            rows = pl.ds(pl.multiple_of(at * TILE, TILE), TILE)
            one, two = one_ref[rows, :], two_ref[rows, :]
            for lane in range(unroll):
                part = picked_norm[lane] - inner[:, lane * TILE : (lane + 1) * TILE]
                two = jnp.minimum(two, jnp.maximum(one, part))
                one = jnp.minimum(one, part)
            one_ref[rows, :] = one
            two_ref[rows, :] = two
        return 0

    lax.fori_loop(0, (written + together - 1) // together, step, 0)


def near_kernel(
    lists_ref, norms_in, own_group, near_group, own_frames, frames_1, frames_2,
    out_ref, rows_buf, frames_buf, norms_buf, one_buf, two_buf, table_ref, sems,
):
    tile_rows = own_group.shape[0]
    tiles_here = tile_rows // TILE
    quarter = own_frames.shape[0]
    quarter_tiles = quarter // TILE
    copies = [
        pltpu.make_async_copy(own_group, rows_buf.at[pl.ds(0, tile_rows)], sems.at[0]),
        pltpu.make_async_copy(near_group, rows_buf.at[pl.ds(tile_rows, tile_rows)], sems.at[1]),
    ]
    for index, ref in enumerate((own_frames, frames_1, frames_2)):
        copies.append(
            pltpu.make_async_copy(
                ref, frames_buf.at[pl.ds(index * quarter, quarter)], sems.at[2 + index]
            )
        )
    for copy in copies:
        copy.start()
    norms_buf[pl.ds(0, tiles_here), :] = norms_in[0]
    norms_buf[pl.ds(tiles_here, tiles_here), :] = norms_in[1]
    norms_buf[pl.ds(2 * tiles_here, 1), :] = jnp.full((1, TILE), big_value, jnp.float32)
    for copy in copies:
        copy.wait()
    tiles = 3 * quarter_tiles
    search(
        tiles, (0, 1), 0, quarter_tiles, tiles_here, lists_ref, rows_buf, norms_buf,
        frames_buf, one_buf, two_buf, table_ref,
    )
    for index in range(tiles):
        one, two = row_pair(one_buf[pl.ds(index * TILE, TILE), :], two_buf[pl.ds(index * TILE, TILE), :])
        out_ref[0, index : index + 1, :] = one
        out_ref[1, index : index + 1, :] = two


def far_kernel(
    where_ref, lists_ref, norms_in, before_ref, frame_norms, own_group, near_group,
    far_a, far_b, far_c, last_a, last_b, last_c, own_frames, frames_1, frames_2, frames_3a, frames_3b,
    out_ref, rows_buf, frames_buf, norms_buf, one_buf, two_buf, table_ref, sems,
):
    tile_rows = own_group.shape[0]
    tiles_here = tile_rows // TILE
    groups = norms_in.shape[0]
    quarter = own_frames.shape[0]
    quarter_tiles = quarter // TILE
    width = own_frames.shape[1]
    members = frames_buf.shape[0] // quarter
    member = where_ref[0]
    slab = where_ref[2]
    side = far_a.shape[0]
    middle = far_b.shape[0]
    near_side = slab * (tile_rows - side)
    other_side = (1 - slab) * (tile_rows - side)

    copies = []

    def bring(source, target, start, rows):
        copies.append(
            pltpu.make_async_copy(
                source, target.at[pl.ds(pl.multiple_of(start, TILE), rows)], sems.at[len(copies)]
            )
        )

    for slot, (first_piece, second_piece, third_piece) in (
        (2, (far_a, far_b, far_c)),
        (3, (last_a, last_b, last_c)),
    ):
        bring(first_piece, rows_buf, slot * tile_rows + near_side, side)
        bring(second_piece, rows_buf, slot * tile_rows + side, middle)
        bring(third_piece, rows_buf, slot * tile_rows + other_side, side)
    bring(own_frames, frames_buf, 0, quarter)
    bring(frames_1, frames_buf, quarter, quarter)
    bring(frames_2, frames_buf, 2 * quarter, quarter)
    early = len(copies)
    bring(own_group, rows_buf, 0, tile_rows)
    bring(near_group, rows_buf, tile_rows, tile_rows)
    for copy in copies[:early]:
        copy.start()
    inner_member = jnp.logical_and(member > 0, member < members - 1)
    last_sem = sems.at[len(copies)]
    last_target = frames_buf.at[pl.ds(3 * quarter, quarter)]

    @pl.when(inner_member)
    def _():
        pltpu.make_async_copy(frames_3a, last_target, last_sem).start()

    @pl.when(jnp.logical_not(inner_member))
    def _():
        pltpu.make_async_copy(frames_3b, last_target, last_sem).start()

    for copy in copies[early:]:
        copy.start()

    dummy = groups * tiles_here
    for slot in range(groups):
        norms_buf[pl.ds(slot * tiles_here, tiles_here), :] = norms_in[slot]
    norms_buf[pl.ds(dummy, 1), :] = jnp.full((1, TILE), big_value, jnp.float32)
    for copy in copies[:early]:
        copy.wait()

    def finish(index, at, before_one, before_two, frame_norm):
        rows = pl.ds(at * TILE, TILE)
        one, two = row_pair(one_buf[rows, :], two_buf[rows, :])
        if before_one is not None:
            one, two = fold_two(one, two, before_one, before_two)
        block_of = jnp.bitwise_xor(member, index // quarter_tiles)
        row = block_of * quarter_tiles + index % quarter_tiles
        out_ref[0, pl.ds(row, 1), :] = (frame_norm + 2.0 * one) / width
        out_ref[1, pl.ds(row, 1), :] = (frame_norm + 2.0 * two) / width

    early_tiles = 3 * quarter_tiles
    search(
        early_tiles, (2, 3), 0, quarter_tiles, tiles_here, lists_ref,
        rows_buf.at[pl.ds(2 * tile_rows, 2 * tile_rows)],
        norms_buf.at[pl.ds(2 * tiles_here, 2 * tiles_here + 8)],
        frames_buf, one_buf, two_buf, table_ref,
    )
    for index in range(early_tiles):
        finish(
            index, index, before_ref[0, index : index + 1, :], before_ref[1, index : index + 1, :],
            frame_norms[index : index + 1, :],
        )
    pltpu.make_async_copy(frames_3a, last_target, last_sem).wait()
    for copy in copies[early:]:
        copy.wait()
    search(
        quarter_tiles, tuple(range(groups)), early_tiles, quarter_tiles, tiles_here, lists_ref,
        rows_buf, norms_buf, frames_buf, one_buf, two_buf, table_ref,
    )
    for tile in range(quarter_tiles):
        rows = frames_buf[pl.ds((early_tiles + tile) * TILE, TILE), :].astype(jnp.float32)
        finish(early_tiles + tile, tile, None, None, column_of(rows * rows))


def pick_kernel(where_ref, plan_ref, part_0, part_1, part_2, part_3, first_ref, second_ref, every):
    member = where_ref[0]
    piece = where_ref[1]
    blocks = first_ref.shape[0]
    parts = (part_0, part_1, part_2, part_3)
    quarter_tiles = blocks // len(parts)
    rows = part_0.shape[1]
    for slot, part in enumerate(parts):
        every[:, slot * rows : (slot + 1) * rows, :] = part[...]
    for place in range(blocks):
        tile = plan_ref[member * blocks + place]
        block_of = tile // blocks
        inside = tile - block_of * blocks
        part = inside // quarter_tiles
        row = jnp.bitwise_xor(part, piece) * rows + block_of * quarter_tiles + (inside - part * quarter_tiles)
        first_ref[pl.ds(place, 1), :] = every[0, pl.ds(row, 1), :]
        second_ref[pl.ds(place, 1), :] = every[1, pl.ds(row, 1), :]


def exchanged(number, distance):
    return [(at, at ^ distance) for at in range(number)]


def gathered_frames(frames, medoids, tile_ids, tile_counts, plan):
    width = frames.shape[1]
    blocks = frames.shape[0] // TILE
    members = lax.axis_size("frames")
    groups = lax.axis_size("medoids")
    member = lax.axis_index("frames")
    piece = lax.axis_index("medoids")
    slab = lax.axis_index("slab")
    rows = medoids[0]
    tile_rows = rows.shape[0]
    quarter_tiles = blocks // groups
    quarter = quarter_tiles * TILE
    side = tile_rows // TILE // 3 * TILE

    mine = lax.dynamic_slice_in_dim(frames, piece * quarter, quarter)
    frames_2 = lax.ppermute(mine, "frames", exchanged(members, 2))
    frames_1 = lax.ppermute(mine, "frames", exchanged(members, 1))
    frames_3a = lax.ppermute(mine, "frames", [(1, 2), (2, 1)])
    frames_3b = lax.ppermute(frames_2, "frames", [(2, 3), (1, 0)])

    edge = lax.dynamic_slice_in_dim(rows, slab * (tile_rows - side), side)
    far_a = lax.ppermute(edge, "medoids", exchanged(groups, 2))
    far_b = lax.ppermute(rows[side : tile_rows - side], "medoids", exchanged(groups, 2))
    far_c = lax.ppermute(far_a, "slab", exchanged(2, 1))
    near_group = lax.ppermute(rows, "medoids", exchanged(groups, 1))
    last_a = lax.ppermute(far_a, "medoids", exchanged(groups, 1))
    last_b = lax.ppermute(far_b, "medoids", exchanged(groups, 1))
    last_c = lax.ppermute(far_c, "medoids", exchanged(groups, 1))

    tiles_here = tile_rows // TILE
    where = jnp.stack([member, piece, slab, jnp.int32(tiles_here)]).astype(jnp.int32)
    hbm = pl.BlockSpec(memory_space=pl.ANY)
    scalar = pl.BlockSpec(memory_space=pltpu.SMEM)
    vector = pl.BlockSpec(memory_space=pltpu.VMEM)
    lanes = TILE // members
    listed = pl.pallas_call(
        functools.partial(split_kernel, members),
        out_shape=jax.ShapeDtypeStruct((blocks, members * lanes), jnp.int32),
        in_specs=[scalar] * 3,
        out_specs=scalar,
        compiler_params=pltpu.CompilerParams(vmem_limit_bytes=small_vmem),
        name="split",
    )(where, tile_ids[0], tile_counts)
    pair = jnp.stack([listed, lax.ppermute(listed, "medoids", exchanged(groups, 1))])
    far_pair = lax.ppermute(pair, "medoids", exchanged(groups, 2))
    lists = jnp.concatenate([pair, far_pair], axis=0)
    lists = lax.dynamic_slice_in_dim(lists, piece * quarter_tiles, quarter_tiles, axis=1)
    lists = lists.reshape(groups, quarter_tiles, members, lanes)
    lists = jnp.stack(
        [lists[:, :, 0]]
        + [lax.ppermute(lists[:, :, at], "frames", exchanged(members, at)) for at in (1, 2, 3)]
    )
    norms = pl.pallas_call(
        functools.partial(norms_kernel, 0.5),
        out_shape=jax.ShapeDtypeStruct((tiles_here, TILE), jnp.float32),
        in_specs=[vector],
        out_specs=vector,
        compiler_params=pltpu.CompilerParams(vmem_limit_bytes=small_vmem),
        name="medoid_norms",
    )(rows)
    norm_pair = jnp.stack([norms, lax.ppermute(norms, "medoids", exchanged(groups, 1))])
    norm_far = lax.ppermute(norm_pair, "medoids", exchanged(groups, 2))
    norms = jnp.concatenate([norm_pair, norm_far], axis=0)
    frame_norms = pl.pallas_call(
        functools.partial(norms_kernel, 1.0),
        out_shape=jax.ShapeDtypeStruct((3 * quarter_tiles, TILE), jnp.float32),
        in_specs=[vector] * 3,
        out_specs=vector,
        compiler_params=pltpu.CompilerParams(vmem_limit_bytes=small_vmem),
        name="frame_norms",
    )(mine, frames_1, frames_2)

    total_tiles = members * quarter_tiles
    early_tiles = 3 * quarter_tiles
    table_size = early_tiles * (groups * tile_ids.shape[2] // unroll + 1) + together
    before = pl.pallas_call(
        near_kernel,
        out_shape=jax.ShapeDtypeStruct((2, early_tiles, TILE), jnp.float32),
        in_specs=[scalar, vector] + [hbm] * 5,
        out_specs=vector,
        scratch_shapes=[
            pltpu.VMEM((2 * tile_rows, width), jnp.bfloat16),
            pltpu.VMEM((3 * quarter, width), jnp.bfloat16),
            pltpu.VMEM((2 * tiles_here + 8, TILE), jnp.float32),
            pltpu.VMEM((3 * quarter, TILE), jnp.float32),
            pltpu.VMEM((3 * quarter, TILE), jnp.float32),
            pltpu.SMEM((table_size,), jnp.int32),
            pltpu.SemaphoreType.DMA((5,)),
        ],
        compiler_params=pltpu.CompilerParams(vmem_limit_bytes=large_vmem),
        name="near_search",
    )(lists, norm_pair, rows, near_group, mine, frames_1, frames_2)
    found = pl.pallas_call(
        far_kernel,
        out_shape=jax.ShapeDtypeStruct((2, total_tiles, TILE), jnp.float32),
        in_specs=[scalar, scalar, vector, vector, vector] + [hbm] * 13,
        out_specs=vector,
        scratch_shapes=[
            pltpu.VMEM((groups * tile_rows, width), jnp.bfloat16),
            pltpu.VMEM((members * quarter, width), jnp.bfloat16),
            pltpu.VMEM((groups * tiles_here + 8, TILE), jnp.float32),
            pltpu.VMEM((3 * quarter, TILE), jnp.float32),
            pltpu.VMEM((3 * quarter, TILE), jnp.float32),
            pltpu.SMEM((table_size,), jnp.int32),
            pltpu.SemaphoreType.DMA((16,)),
        ],
        compiler_params=pltpu.CompilerParams(vmem_limit_bytes=large_vmem),
        name="far_search",
    )(
        where, lists, norms, before, frame_norms, rows, near_group,
        far_a, far_b, far_c, last_a, last_b, last_c, mine, frames_1, frames_2, frames_3a, frames_3b,
    )

    one, two = found[0], found[1]
    for at in (1, 2, 3):
        other = lax.ppermute(found, "frames", exchanged(members, at))
        one, two = fold_two(one, two, other[0], other[1])
    merged = jnp.stack([one, two])
    parts = [merged] + [lax.ppermute(merged, "medoids", exchanged(groups, at)) for at in (1, 2, 3)]
    first, second = pl.pallas_call(
        pick_kernel,
        out_shape=(jax.ShapeDtypeStruct((blocks, TILE), jnp.float32),) * 2,
        in_specs=[scalar, scalar] + [vector] * 4,
        out_specs=(vector, vector),
        scratch_shapes=[pltpu.VMEM((2, groups * members * quarter_tiles, TILE), jnp.float32)],
        compiler_params=pltpu.CompilerParams(vmem_limit_bytes=small_vmem),
        name="pick",
    )(where, plan, *parts)
    return (first.reshape(-1), second.reshape(-1))


def solution(mesh):
    placed = (
        P(("slab", "frames"), None),
        P("medoids", "frames", None),
        P("medoids", ("slab", "frames"), None),
        P("medoids", ("slab", "frames")),
        P("slab"),
    )

    def per_device(frames, medoids, tile_ids, tile_counts, plan):
        blocks = frames.shape[0] // TILE
        quarters = mesh.shape["frames"] == 4 and mesh.shape["medoids"] == 4 and mesh.shape["slab"] == 2
        if quarters and blocks % 4 == 0 and medoids.shape[1] // TILE >= 3:
            return gathered_frames(frames, medoids, tile_ids, tile_counts, plan)
        return gathered_medoids(frames, medoids, tile_ids, tile_counts, plan)

    return jax.shard_map(
        per_device,
        mesh=mesh,
        in_specs=placed,
        out_specs=(P(("slab", "frames")), P(("slab", "frames"))),
        check_vma=False,
    )
```

```python
import functools

import jax
import jax.numpy as jnp
from jax import lax
from jax.experimental import pallas as pl
from jax.experimental.pallas import tpu as pltpu
from jax.sharding import PartitionSpec as P


TILE = 128


big_value = 1e30
per_block = 8
unroll = 2
together = 6
small_vmem = 8 << 20
large_vmem = 24 << 20
whole_vmem = 61 << 20


def fold_two(left_one, left_two, right_one, right_two):
    first = jnp.minimum(left_one, right_one)
    second = jnp.minimum(jnp.maximum(left_one, right_one), jnp.minimum(left_two, right_two))
    return (first, second)


def tile_pass(frame_tile, ids, count, group_rows, group_norm):
    width = frame_tile.shape[1]
    rows_tile = frame_tile.shape[0]
    frame_norm = jnp.sum(jnp.square(frame_tile.astype(jnp.float32)), axis=1)

    def step(block, carry):
        start = (block * per_block).astype(jnp.int32)
        chosen = lax.dynamic_slice_in_dim(ids, start, per_block)
        live = start + jnp.arange(per_block, dtype=jnp.int32) < count
        rows = group_rows[chosen].reshape(per_block * rows_tile, width)
        norms = group_norm[chosen].reshape(per_block * rows_tile)
        inner = lax.dot_general(
            frame_tile, rows, (((1,), (1,)), ((), ())), preferred_element_type=jnp.float32
        )
        dist = (frame_norm[:, None] + norms[None, :] - 2.0 * inner) / width
        keep = jnp.repeat(live, rows_tile)
        dist = jnp.where(keep[None, :], dist, jnp.float32(big_value))
        lowest = -lax.top_k(-dist, 2)[0]
        return fold_two(carry[0], carry[1], lowest[:, 0], lowest[:, 1])

    start_pair = (
        jnp.full((rows_tile,), big_value, jnp.float32),
        jnp.full((rows_tile,), big_value, jnp.float32),
    )
    blocks = (count + per_block - 1) // per_block
    return lax.fori_loop(0, blocks, step, start_pair)


def all_tiles(tiles, ids, counts, group_rows, group_norm):
    number = tiles.shape[0]

    def one_tile(index, carry):
        found_one, found_two = tile_pass(
            tiles[index], ids[index], counts[index], group_rows, group_norm
        )
        return (carry[0].at[index].set(found_one), carry[1].at[index].set(found_two))

    empty = jnp.zeros((number, TILE), jnp.float32)
    return lax.fori_loop(0, number, one_tile, (empty, empty))


def across_groups(first, second):
    every_one, every_two = (
        lax.all_gather(first[None], "medoids", axis=0, tiled=True),
        lax.all_gather(second[None], "medoids", axis=0, tiled=True),
    )
    best_one, best_two = (every_one[0], every_two[0])
    for group in range(1, every_one.shape[0]):
        best_one, best_two = fold_two(best_one, best_two, every_one[group], every_two[group])
    return (best_one, best_two)


def gathered_medoids(frames, medoids, tile_ids, tile_counts, plan):
    width = frames.shape[1]
    blocks = frames.shape[0] // TILE
    members = lax.axis_size("frames")
    member = lax.axis_index("frames")
    capacity = (blocks + members - 1) // members
    group = lax.all_gather(medoids[0], "frames", axis=0, tiled=True)
    group_tiles = group.shape[0] // TILE
    group_rows = group.reshape(group_tiles, TILE, width)
    group_norm = jnp.sum(jnp.square(group.astype(jnp.float32)), axis=1).reshape(group_tiles, TILE)
    total = plan.shape[0]
    position = jnp.zeros((total,), jnp.int32).at[plan].set(jnp.arange(total, dtype=jnp.int32))
    target = (position // blocks).reshape(members, blocks)
    matching = target[:, :, None] == target[:, None, :]
    earlier = jnp.arange(blocks)[None, :] < jnp.arange(blocks)[:, None]
    slot_table = jnp.sum(jnp.logical_and(matching, earlier[None]), axis=2)
    my_target = lax.dynamic_index_in_dim(target, member, 0, keepdims=False)
    my_slot = lax.dynamic_index_in_dim(slot_table, member, 0, keepdims=False)
    arriving = lax.dynamic_slice_in_dim(plan, member * blocks, blocks)
    sender = arriving // blocks
    sender_slot = slot_table.reshape(-1)[arriving]
    tiles = frames.reshape(blocks, TILE, width)
    outgoing_tiles = (
        jnp.zeros((members, capacity, TILE, width), frames.dtype).at[my_target, my_slot].set(tiles)
    )
    outgoing_ids = (
        jnp.zeros((members, capacity, tile_ids.shape[2]), jnp.int32)
        .at[my_target, my_slot]
        .set(tile_ids[0])
    )
    outgoing_counts = (
        jnp.zeros((members, capacity), jnp.int32).at[my_target, my_slot].set(tile_counts[0])
    )
    incoming_tiles, incoming_ids, incoming_counts = (
        lax.all_to_all(outgoing_tiles, "frames", split_axis=0, concat_axis=0, tiled=True),
        lax.all_to_all(outgoing_ids, "frames", split_axis=0, concat_axis=0, tiled=True),
        lax.all_to_all(outgoing_counts, "frames", split_axis=0, concat_axis=0, tiled=True),
    )
    placed_tiles = incoming_tiles[sender, sender_slot]
    placed_ids = incoming_ids[sender, sender_slot]
    placed_counts = incoming_counts[sender, sender_slot]
    first, second = all_tiles(placed_tiles, placed_ids, placed_counts, group_rows, group_norm)
    first, second = across_groups(first, second)
    return (first.reshape(-1), second.reshape(-1))


def column_of(squares):
    total = squares[:, 0:TILE]
    for at_lane in range(TILE, squares.shape[1], TILE):
        total = total + squares[:, at_lane : at_lane + TILE]
    return jnp.sum(total.T, axis=0, keepdims=True)


def row_pair(one, two):
    one, two = one.T, two.T
    rows = one.shape[0]
    while rows > 8:
        half = rows // 2
        one, two = fold_two(one[:half], two[:half], one[half:], two[half:])
        rows = half
    for shift in (4, 2, 1):
        one, two = fold_two(one, two, pltpu.roll(one, shift, 0), pltpu.roll(two, shift, 0))
    return one[0:1], two[0:1]


def cut_kernel(frames_ref, group_ref, mine_ref, edge_ref, middle_ref, sems):
    quarter = mine_ref.shape[0]
    side = edge_ref.shape[0]
    piece = pl.multiple_of(lax.axis_index("medoids") * quarter, TILE)
    end = pl.multiple_of(lax.axis_index("slab") * (group_ref.shape[0] - side), TILE)
    copies = (
        pltpu.make_async_copy(frames_ref.at[pl.ds(piece, quarter)], mine_ref, sems.at[0]),
        pltpu.make_async_copy(group_ref.at[pl.ds(end, side)], edge_ref, sems.at[1]),
        pltpu.make_async_copy(
            group_ref.at[pl.ds(side, middle_ref.shape[0])], middle_ref, sems.at[2]
        ),
    )
    for copy in copies:
        copy.start()
    for copy in copies:
        copy.wait()


def split_kernel(members, tiles_here, ids_ref, lists_ref):
    member = lax.axis_index("frames")
    rows, columns = ids_ref.shape
    lanes = lists_ref.shape[1] // members
    shape = (rows, members * lanes)
    lane = lax.broadcasted_iota(jnp.int32, shape, 1)
    distance = lane // lanes
    within = lane - distance * lanes
    shard = jnp.bitwise_xor(distance, member)
    low = shard * tiles_here
    count = jnp.broadcast_to(ids_ref[:, columns - 1 : columns], shape)
    taken = jnp.zeros(shape, jnp.int32)
    lists = jnp.zeros(shape, jnp.int32)
    for at in range(columns - 1):
        entry = jnp.broadcast_to(ids_ref[:, at : at + 1], shape) - low
        here = (entry >= 0) & (entry < tiles_here) & (at < count)
        lists = jnp.where(here & (within == taken), entry, lists)
        taken = taken + here.astype(jnp.int32)
    lists_ref[...] = jnp.where(within == lanes - 1, taken, lists)


def route_kernel(own_ref, near_ref, far_ref, out_ref):
    quarter_tiles = out_ref.shape[0] // 4
    start = lax.axis_index("medoids") * quarter_tiles
    for slot, ref in enumerate((own_ref, near_ref, far_ref.at[0], far_ref.at[1])):
        for tile in range(quarter_tiles):
            row = slot * quarter_tiles + tile
            out_ref[row : row + 1, :] = ref[pl.ds(start + tile, 1), :]


def norms_kernel(scale, *refs):
    norms_ref = refs[-1]
    row = 0
    for ref in refs[:-1]:
        for tile in range(ref.shape[0] // TILE):
            rows = ref[tile * TILE : (tile + 1) * TILE, :].astype(jnp.float32)
            norms_ref[row : row + 1, :] = scale * column_of(rows * rows)
            row += 1


def search(
    tiles, slots, first_tile, quarter_tiles, tiles_here, lists_ref, rows_ref, norms_ref,
    frames_ref, one_ref, two_ref, table_ref,
):
    lanes = lists_ref.shape[2] // lists_ref.shape[0]
    dummy = len(slots) * tiles_here
    shift = 16

    def listed(zslot, slot, tile, place):
        return lists_ref[zslot, slot * quarter_tiles + tile, zslot * lanes + place]

    def place_of(index):
        zslot = index // quarter_tiles
        return zslot, index - zslot * quarter_tiles

    def ends_of(index):
        zslot, tile = place_of(index)
        ends, number = [], jnp.int32(0)
        for slot in slots:
            number = number + listed(zslot, slot, tile, lanes - 1)
            ends.append(number)
        return ends

    def blocks_of(at, written):
        blocks = (ends_of(first_tile + at)[-1] + unroll - 1) // unroll

        def put(block, _):
            table_ref[written + block] = (block << shift) + at
            return 0

        lax.fori_loop(0, blocks, put, 0)
        return written + blocks

    written = lax.fori_loop(0, tiles, blocks_of, jnp.int32(0))
    for extra in range(together - 1):
        table_ref[written + extra] = jnp.int32(1 << (shift + 8))
    size = tiles * TILE
    one_ref[0:size, :] = jnp.full((size, TILE), big_value, jnp.float32)
    two_ref[0:size, :] = jnp.full((size, TILE), big_value, jnp.float32)

    def step(at_step, _):
        results = []
        for member in range(together):
            code = table_ref[at_step * together + member]
            at = jnp.bitwise_and(code, (1 << shift) - 1)
            block = code >> shift
            index = first_tile + at
            zslot, tile = place_of(index)
            ends = ends_of(index)
            picked, picked_norm = [], []
            for lane in range(unroll):
                place = block * unroll + lane
                live = place < ends[-1]
                slot, start = jnp.int32(0), jnp.int32(0)
                for number in range(1, len(slots)):
                    beyond = place >= ends[number - 1]
                    slot = jnp.where(beyond, number, slot)
                    start = jnp.where(beyond, ends[number - 1], start)
                place = jnp.where(live, place - start, 0)
                entry = listed(zslot, slots[0] + slot, tile, place) + slot * tiles_here
                row = jnp.where(live, entry, 0) * TILE
                picked.append(rows_ref[pl.ds(pl.multiple_of(row, TILE), TILE), :])
                picked_norm.append(norms_ref[pl.ds(jnp.where(live, entry, dummy), 1), :])
            inner = lax.dot_general(
                frames_ref[pl.ds(pl.multiple_of(index * TILE, TILE), TILE), :],
                jnp.concatenate(picked, axis=0),
                (((1,), (1,)), ((), ())),
                preferred_element_type=jnp.float32,
            )
            results.append((at, picked_norm, inner))
        for at, picked_norm, inner in results:
            rows = pl.ds(pl.multiple_of(at * TILE, TILE), TILE)
            one, two = one_ref[rows, :], two_ref[rows, :]
            for lane in range(unroll):
                part = picked_norm[lane] - inner[:, lane * TILE : (lane + 1) * TILE]
                two = jnp.minimum(two, jnp.maximum(one, part))
                one = jnp.minimum(one, part)
            one_ref[rows, :] = one
            two_ref[rows, :] = two
        return 0

    lax.fori_loop(0, (written + together - 1) // together, step, 0)


def near_kernel(
    lists_0, lists_1, lists_2, lists_3, norms_own, norms_near, own_group, near_group,
    own_frames, frames_1, frames_2,
    out_ref, lists_ref, rows_buf, frames_buf, norms_buf, one_buf, two_buf, table_ref, sems,
):
    tile_rows = own_group.shape[0]
    tiles_here = tile_rows // TILE
    quarter = own_frames.shape[0]
    quarter_tiles = quarter // TILE
    copies = [
        pltpu.make_async_copy(own_group, rows_buf.at[pl.ds(0, tile_rows)], sems.at[0]),
        pltpu.make_async_copy(near_group, rows_buf.at[pl.ds(tile_rows, tile_rows)], sems.at[1]),
    ]
    for index, ref in enumerate((own_frames, frames_1, frames_2)):
        copies.append(
            pltpu.make_async_copy(
                ref, frames_buf.at[pl.ds(index * quarter, quarter)], sems.at[2 + index]
            )
        )
    for index, ref in enumerate((lists_0, lists_1, lists_2, lists_3)):
        copies.append(pltpu.make_async_copy(ref, lists_ref.at[index], sems.at[5 + index]))
    for copy in copies:
        copy.start()
    norms_buf[pl.ds(0, tiles_here), :] = norms_own[...]
    norms_buf[pl.ds(tiles_here, tiles_here), :] = norms_near[...]
    norms_buf[pl.ds(2 * tiles_here, 1), :] = jnp.full((1, TILE), big_value, jnp.float32)
    for copy in copies:
        copy.wait()
    tiles = 3 * quarter_tiles
    search(
        tiles, (0, 1), 0, quarter_tiles, tiles_here, lists_ref, rows_buf, norms_buf,
        frames_buf, one_buf, two_buf, table_ref,
    )
    for index in range(tiles):
        one, two = row_pair(one_buf[pl.ds(index * TILE, TILE), :], two_buf[pl.ds(index * TILE, TILE), :])
        out_ref[0, index : index + 1, :] = one
        out_ref[1, index : index + 1, :] = two


def far_kernel(
    lists_0, lists_1, lists_2, lists_3, norms_own, norms_near, norms_far, before_ref, frame_norms,
    own_group, near_group, far_a, far_b, far_c, last_a, last_b, last_c,
    own_frames, frames_1, frames_2, frames_3a, frames_3b,
    out_ref, lists_ref, rows_buf, frames_buf, norms_buf, one_buf, two_buf, table_ref, sems,
):
    tile_rows = own_group.shape[0]
    tiles_here = tile_rows // TILE
    groups = 2 + norms_far.shape[0]
    quarter = own_frames.shape[0]
    quarter_tiles = quarter // TILE
    width = own_frames.shape[1]
    members = frames_buf.shape[0] // quarter
    member = lax.axis_index("frames")
    slab = lax.axis_index("slab")
    side = far_a.shape[0]
    middle = far_b.shape[0]
    near_side = slab * (tile_rows - side)
    other_side = (1 - slab) * (tile_rows - side)

    copies = []

    def bring(source, target, start, rows):
        copies.append(
            pltpu.make_async_copy(
                source, target.at[pl.ds(pl.multiple_of(start, TILE), rows)], sems.at[len(copies)]
            )
        )

    for slot, (first_piece, second_piece, third_piece) in (
        (2, (far_a, far_b, far_c)),
        (3, (last_a, last_b, last_c)),
    ):
        bring(first_piece, rows_buf, slot * tile_rows + near_side, side)
        bring(second_piece, rows_buf, slot * tile_rows + side, middle)
        bring(third_piece, rows_buf, slot * tile_rows + other_side, side)
    bring(own_frames, frames_buf, 0, quarter)
    bring(frames_1, frames_buf, quarter, quarter)
    bring(frames_2, frames_buf, 2 * quarter, quarter)
    for index, ref in enumerate((lists_0, lists_1, lists_2, lists_3)):
        copies.append(pltpu.make_async_copy(ref, lists_ref.at[index], sems.at[len(copies)]))
    early = len(copies)
    bring(own_group, rows_buf, 0, tile_rows)
    bring(near_group, rows_buf, tile_rows, tile_rows)
    for copy in copies[:early]:
        copy.start()
    inner_member = jnp.logical_and(member > 0, member < members - 1)
    last_sem = sems.at[len(copies)]
    last_target = frames_buf.at[pl.ds(3 * quarter, quarter)]

    @pl.when(inner_member)
    def _():
        pltpu.make_async_copy(frames_3a, last_target, last_sem).start()

    @pl.when(jnp.logical_not(inner_member))
    def _():
        pltpu.make_async_copy(frames_3b, last_target, last_sem).start()

    for copy in copies[early:]:
        copy.start()

    dummy = groups * tiles_here
    for slot, norms in enumerate((norms_own, norms_near, norms_far.at[0], norms_far.at[1])):
        norms_buf[pl.ds(slot * tiles_here, tiles_here), :] = norms[...]
    norms_buf[pl.ds(dummy, 1), :] = jnp.full((1, TILE), big_value, jnp.float32)
    for copy in copies[:early]:
        copy.wait()

    def finish(index, at, before_one, before_two, frame_norm):
        rows = pl.ds(at * TILE, TILE)
        one, two = row_pair(one_buf[rows, :], two_buf[rows, :])
        if before_one is not None:
            one, two = fold_two(one, two, before_one, before_two)
        block_of = jnp.bitwise_xor(member, index // quarter_tiles)
        row = block_of * quarter_tiles + index % quarter_tiles
        out_ref[0, pl.ds(row, 1), :] = (frame_norm + 2.0 * one) / width
        out_ref[1, pl.ds(row, 1), :] = (frame_norm + 2.0 * two) / width

    early_tiles = 3 * quarter_tiles
    search(
        early_tiles, (2, 3), 0, quarter_tiles, tiles_here, lists_ref,
        rows_buf.at[pl.ds(2 * tile_rows, 2 * tile_rows)],
        norms_buf.at[pl.ds(2 * tiles_here, 2 * tiles_here + 8)],
        frames_buf, one_buf, two_buf, table_ref,
    )
    for index in range(early_tiles):
        finish(
            index, index, before_ref[0, index : index + 1, :], before_ref[1, index : index + 1, :],
            frame_norms[index : index + 1, :],
        )
    pltpu.make_async_copy(frames_3a, last_target, last_sem).wait()
    for copy in copies[early:]:
        copy.wait()
    search(
        quarter_tiles, tuple(range(groups)), early_tiles, quarter_tiles, tiles_here, lists_ref,
        rows_buf, norms_buf, frames_buf, one_buf, two_buf, table_ref,
    )
    for tile in range(quarter_tiles):
        rows = frames_buf[pl.ds((early_tiles + tile) * TILE, TILE), :].astype(jnp.float32)
        finish(early_tiles + tile, tile, None, None, column_of(rows * rows))


def pick_kernel(plan_ref, part_0, part_1, part_2, part_3, first_ref, second_ref, every):
    member = lax.axis_index("frames")
    piece = lax.axis_index("medoids")
    blocks = first_ref.shape[0]
    parts = (part_0, part_1, part_2, part_3)
    quarter_tiles = blocks // len(parts)
    rows = part_0.shape[1]
    for slot, part in enumerate(parts):
        every[:, slot * rows : (slot + 1) * rows, :] = part[...]
    for place in range(blocks):
        tile = plan_ref[member * blocks + place]
        block_of = tile // blocks
        inside = tile - block_of * blocks
        part = inside // quarter_tiles
        row = jnp.bitwise_xor(part, piece) * rows + block_of * quarter_tiles + (inside - part * quarter_tiles)
        first_ref[pl.ds(place, 1), :] = every[0, pl.ds(row, 1), :]
        second_ref[pl.ds(place, 1), :] = every[1, pl.ds(row, 1), :]


def exchanged(number, distance):
    return [(at, at ^ distance) for at in range(number)]


def gathered_frames(frames, medoids, tile_ids, tile_counts, plan):
    width = frames.shape[1]
    blocks = frames.shape[0] // TILE
    members = lax.axis_size("frames")
    groups = lax.axis_size("medoids")
    rows = medoids[0]
    tile_rows = rows.shape[0]
    quarter_tiles = blocks // groups
    quarter = quarter_tiles * TILE
    side = tile_rows // TILE // 3 * TILE

    hbm = pl.BlockSpec(memory_space=pl.ANY)
    scalar = pl.BlockSpec(memory_space=pltpu.SMEM)
    vector = pl.BlockSpec(memory_space=pltpu.VMEM)
    small = pltpu.CompilerParams(vmem_limit_bytes=small_vmem)
    large = pltpu.CompilerParams(vmem_limit_bytes=large_vmem)
    mine, edge, inside_rows = pl.pallas_call(
        cut_kernel,
        out_shape=(
            jax.ShapeDtypeStruct((quarter, width), frames.dtype),
            jax.ShapeDtypeStruct((side, width), rows.dtype),
            jax.ShapeDtypeStruct((tile_rows - 2 * side, width), rows.dtype),
        ),
        in_specs=[hbm, hbm],
        out_specs=(vector, vector, vector),
        scratch_shapes=[pltpu.SemaphoreType.DMA((3,))],
        compiler_params=pltpu.CompilerParams(vmem_limit_bytes=whole_vmem),
        name="cut",
    )(frames, rows)
    frames_2 = lax.ppermute(mine, "frames", exchanged(members, 2))
    frames_1 = lax.ppermute(mine, "frames", exchanged(members, 1))
    frames_3a = lax.ppermute(mine, "frames", [(1, 2), (2, 1)])
    frames_3b = lax.ppermute(frames_2, "frames", [(2, 3), (1, 0)])

    far_a = lax.ppermute(edge, "medoids", exchanged(groups, 2))
    far_b = lax.ppermute(inside_rows, "medoids", exchanged(groups, 2))
    far_c = lax.ppermute(far_a, "slab", exchanged(2, 1))
    near_group = lax.ppermute(rows, "medoids", exchanged(groups, 1))
    last_a = lax.ppermute(far_a, "medoids", exchanged(groups, 1))
    last_b = lax.ppermute(far_b, "medoids", exchanged(groups, 1))
    last_c = lax.ppermute(far_c, "medoids", exchanged(groups, 1))

    tiles_here = tile_rows // TILE
    listed = pl.pallas_call(
        functools.partial(split_kernel, members, tiles_here),
        out_shape=jax.ShapeDtypeStruct((blocks, TILE), jnp.int32),
        in_specs=[vector],
        out_specs=vector,
        compiler_params=small,
        name="split",
    )(jnp.concatenate([tile_ids[0], tile_counts[0][:, None]], axis=1))
    near_listed = lax.ppermute(listed, "medoids", exchanged(groups, 1))
    far_listed = lax.ppermute(jnp.stack([listed, near_listed]), "medoids", exchanged(groups, 2))
    lists = pl.pallas_call(
        route_kernel,
        out_shape=jax.ShapeDtypeStruct((groups * quarter_tiles, TILE), jnp.int32),
        in_specs=[vector] * 3,
        out_specs=vector,
        compiler_params=small,
        name="route",
    )(listed, near_listed, far_listed)
    lists = [lists] + [lax.ppermute(lists, "frames", exchanged(members, at)) for at in (1, 2, 3)]
    norms = pl.pallas_call(
        functools.partial(norms_kernel, 0.5),
        out_shape=jax.ShapeDtypeStruct((tiles_here, TILE), jnp.float32),
        in_specs=[vector],
        out_specs=vector,
        compiler_params=small,
        name="medoid_norms",
    )(rows)
    norm_near = lax.ppermute(norms, "medoids", exchanged(groups, 1))
    norm_far = lax.ppermute(jnp.stack([norms, norm_near]), "medoids", exchanged(groups, 2))
    frame_norms = pl.pallas_call(
        functools.partial(norms_kernel, 1.0),
        out_shape=jax.ShapeDtypeStruct((3 * quarter_tiles, TILE), jnp.float32),
        in_specs=[vector] * 3,
        out_specs=vector,
        compiler_params=small,
        name="frame_norms",
    )(mine, frames_1, frames_2)

    total_tiles = members * quarter_tiles
    early_tiles = 3 * quarter_tiles
    table_size = early_tiles * (groups * tile_ids.shape[2] // unroll + 1) + together
    before = pl.pallas_call(
        near_kernel,
        out_shape=jax.ShapeDtypeStruct((2, early_tiles, TILE), jnp.float32),
        in_specs=[hbm] * 4 + [vector] * 2 + [hbm] * 5,
        out_specs=vector,
        scratch_shapes=[
            pltpu.SMEM((members, groups * quarter_tiles, TILE), jnp.int32),
            pltpu.VMEM((2 * tile_rows, width), jnp.bfloat16),
            pltpu.VMEM((3 * quarter, width), jnp.bfloat16),
            pltpu.VMEM((2 * tiles_here + 8, TILE), jnp.float32),
            pltpu.VMEM((3 * quarter, TILE), jnp.float32),
            pltpu.VMEM((3 * quarter, TILE), jnp.float32),
            pltpu.SMEM((table_size,), jnp.int32),
            pltpu.SemaphoreType.DMA((9,)),
        ],
        compiler_params=large,
        name="near_search",
    )(*lists, norms, norm_near, rows, near_group, mine, frames_1, frames_2)
    found = pl.pallas_call(
        far_kernel,
        out_shape=jax.ShapeDtypeStruct((2, total_tiles, TILE), jnp.float32),
        in_specs=[hbm] * 4 + [vector] * 5 + [hbm] * 13,
        out_specs=vector,
        scratch_shapes=[
            pltpu.SMEM((members, groups * quarter_tiles, TILE), jnp.int32),
            pltpu.VMEM((groups * tile_rows, width), jnp.bfloat16),
            pltpu.VMEM((members * quarter, width), jnp.bfloat16),
            pltpu.VMEM((groups * tiles_here + 8, TILE), jnp.float32),
            pltpu.VMEM((3 * quarter, TILE), jnp.float32),
            pltpu.VMEM((3 * quarter, TILE), jnp.float32),
            pltpu.SMEM((table_size,), jnp.int32),
            pltpu.SemaphoreType.DMA((20,)),
        ],
        compiler_params=large,
        name="far_search",
    )(
        *lists, norms, norm_near, norm_far, before, frame_norms, rows, near_group,
        far_a, far_b, far_c, last_a, last_b, last_c, mine, frames_1, frames_2, frames_3a, frames_3b,
    )

    one, two = found[0], found[1]
    for at in (1, 2, 3):
        other = lax.ppermute(found, "frames", exchanged(members, at))
        one, two = fold_two(one, two, other[0], other[1])
    merged = jnp.stack([one, two])
    parts = [merged] + [lax.ppermute(merged, "medoids", exchanged(groups, at)) for at in (1, 2, 3)]
    first, second = pl.pallas_call(
        pick_kernel,
        out_shape=(jax.ShapeDtypeStruct((blocks, TILE), jnp.float32),) * 2,
        in_specs=[scalar] + [vector] * 4,
        out_specs=(vector, vector),
        scratch_shapes=[pltpu.VMEM((2, groups * members * quarter_tiles, TILE), jnp.float32)],
        compiler_params=small,
        name="pick",
    )(plan, *parts)
    return (first.reshape(-1), second.reshape(-1))


def solution(mesh):
    placed = (
        P(("slab", "frames"), None),
        P("medoids", "frames", None),
        P("medoids", ("slab", "frames"), None),
        P("medoids", ("slab", "frames")),
        P("slab"),
    )

    def per_device(frames, medoids, tile_ids, tile_counts, plan):
        blocks = frames.shape[0] // TILE
        quarters = mesh.shape["frames"] == 4 and mesh.shape["medoids"] == 4 and mesh.shape["slab"] == 2
        if quarters and blocks % 4 == 0 and medoids.shape[1] // TILE >= 3:
            return gathered_frames(frames, medoids, tile_ids, tile_counts, plan)
        return gathered_medoids(frames, medoids, tile_ids, tile_counts, plan)

    return jax.shard_map(
        per_device,
        mesh=mesh,
        in_specs=placed,
        out_specs=(P(("slab", "frames")), P(("slab", "frames"))),
        check_vma=False,
    )
```

```python
import functools

import jax
import jax.numpy as jnp
from jax import lax
from jax.experimental import pallas as pl
from jax.experimental.pallas import tpu as pltpu
from jax.sharding import PartitionSpec as P


TILE = 128


big_value = 1e30
per_block = 8
unroll = 2
together = 6
small_vmem = 8 << 20
large_vmem = 24 << 20
whole_vmem = 125 << 19


def fold_two(left_one, left_two, right_one, right_two):
    first = jnp.minimum(left_one, right_one)
    second = jnp.minimum(jnp.maximum(left_one, right_one), jnp.minimum(left_two, right_two))
    return (first, second)


def tile_pass(frame_tile, ids, count, group_rows, group_norm):
    width = frame_tile.shape[1]
    rows_tile = frame_tile.shape[0]
    frame_norm = jnp.sum(jnp.square(frame_tile.astype(jnp.float32)), axis=1)

    def step(block, carry):
        start = (block * per_block).astype(jnp.int32)
        chosen = lax.dynamic_slice_in_dim(ids, start, per_block)
        live = start + jnp.arange(per_block, dtype=jnp.int32) < count
        rows = group_rows[chosen].reshape(per_block * rows_tile, width)
        norms = group_norm[chosen].reshape(per_block * rows_tile)
        inner = lax.dot_general(
            frame_tile, rows, (((1,), (1,)), ((), ())), preferred_element_type=jnp.float32
        )
        dist = (frame_norm[:, None] + norms[None, :] - 2.0 * inner) / width
        keep = jnp.repeat(live, rows_tile)
        dist = jnp.where(keep[None, :], dist, jnp.float32(big_value))
        lowest = -lax.top_k(-dist, 2)[0]
        return fold_two(carry[0], carry[1], lowest[:, 0], lowest[:, 1])

    start_pair = (
        jnp.full((rows_tile,), big_value, jnp.float32),
        jnp.full((rows_tile,), big_value, jnp.float32),
    )
    blocks = (count + per_block - 1) // per_block
    return lax.fori_loop(0, blocks, step, start_pair)


def all_tiles(tiles, ids, counts, group_rows, group_norm):
    number = tiles.shape[0]

    def one_tile(index, carry):
        found_one, found_two = tile_pass(
            tiles[index], ids[index], counts[index], group_rows, group_norm
        )
        return (carry[0].at[index].set(found_one), carry[1].at[index].set(found_two))

    empty = jnp.zeros((number, TILE), jnp.float32)
    return lax.fori_loop(0, number, one_tile, (empty, empty))


def across_groups(first, second):
    every_one, every_two = (
        lax.all_gather(first[None], "medoids", axis=0, tiled=True),
        lax.all_gather(second[None], "medoids", axis=0, tiled=True),
    )
    best_one, best_two = (every_one[0], every_two[0])
    for group in range(1, every_one.shape[0]):
        best_one, best_two = fold_two(best_one, best_two, every_one[group], every_two[group])
    return (best_one, best_two)


def gathered_medoids(frames, medoids, tile_ids, tile_counts, plan):
    width = frames.shape[1]
    blocks = frames.shape[0] // TILE
    members = lax.axis_size("frames")
    member = lax.axis_index("frames")
    capacity = (blocks + members - 1) // members
    group = lax.all_gather(medoids[0], "frames", axis=0, tiled=True)
    group_tiles = group.shape[0] // TILE
    group_rows = group.reshape(group_tiles, TILE, width)
    group_norm = jnp.sum(jnp.square(group.astype(jnp.float32)), axis=1).reshape(group_tiles, TILE)
    total = plan.shape[0]
    position = jnp.zeros((total,), jnp.int32).at[plan].set(jnp.arange(total, dtype=jnp.int32))
    target = (position // blocks).reshape(members, blocks)
    matching = target[:, :, None] == target[:, None, :]
    earlier = jnp.arange(blocks)[None, :] < jnp.arange(blocks)[:, None]
    slot_table = jnp.sum(jnp.logical_and(matching, earlier[None]), axis=2)
    my_target = lax.dynamic_index_in_dim(target, member, 0, keepdims=False)
    my_slot = lax.dynamic_index_in_dim(slot_table, member, 0, keepdims=False)
    arriving = lax.dynamic_slice_in_dim(plan, member * blocks, blocks)
    sender = arriving // blocks
    sender_slot = slot_table.reshape(-1)[arriving]
    tiles = frames.reshape(blocks, TILE, width)
    outgoing_tiles = (
        jnp.zeros((members, capacity, TILE, width), frames.dtype).at[my_target, my_slot].set(tiles)
    )
    outgoing_ids = (
        jnp.zeros((members, capacity, tile_ids.shape[2]), jnp.int32)
        .at[my_target, my_slot]
        .set(tile_ids[0])
    )
    outgoing_counts = (
        jnp.zeros((members, capacity), jnp.int32).at[my_target, my_slot].set(tile_counts[0])
    )
    incoming_tiles, incoming_ids, incoming_counts = (
        lax.all_to_all(outgoing_tiles, "frames", split_axis=0, concat_axis=0, tiled=True),
        lax.all_to_all(outgoing_ids, "frames", split_axis=0, concat_axis=0, tiled=True),
        lax.all_to_all(outgoing_counts, "frames", split_axis=0, concat_axis=0, tiled=True),
    )
    placed_tiles = incoming_tiles[sender, sender_slot]
    placed_ids = incoming_ids[sender, sender_slot]
    placed_counts = incoming_counts[sender, sender_slot]
    first, second = all_tiles(placed_tiles, placed_ids, placed_counts, group_rows, group_norm)
    first, second = across_groups(first, second)
    return (first.reshape(-1), second.reshape(-1))


def column_of(squares):
    total = squares[:, 0:TILE]
    for at_lane in range(TILE, squares.shape[1], TILE):
        total = total + squares[:, at_lane : at_lane + TILE]
    return jnp.sum(total.T, axis=0, keepdims=True)


def row_pair(one, two):
    one, two = one.T, two.T
    rows = one.shape[0]
    while rows > 8:
        half = rows // 2
        one, two = fold_two(one[:half], two[:half], one[half:], two[half:])
        rows = half
    for shift in (4, 2, 1):
        one, two = fold_two(one, two, pltpu.roll(one, shift, 0), pltpu.roll(two, shift, 0))
    return one[0:1], two[0:1]


def cut_first_kernel(frames_ref, group_ref, mine_ref, edge_ref, sems):
    quarter, side = mine_ref.shape[0], edge_ref.shape[0]
    start = pl.multiple_of(lax.axis_index("medoids") * quarter, TILE)
    end = pl.multiple_of(lax.axis_index("slab") * (group_ref.shape[0] - side), TILE)
    copies = start_all(
        (
            (frames_ref.at[pl.ds(start, quarter)], mine_ref),
            (group_ref.at[pl.ds(end, side)], edge_ref),
        ),
        sems,
    )
    for copy in copies:
        copy.wait()


def cut_middle_kernel(side, group_ref, middle_ref, sem):
    copy = pltpu.make_async_copy(group_ref.at[pl.ds(side, middle_ref.shape[0])], middle_ref, sem)
    copy.start()
    copy.wait()


def split_kernel(members, tiles_here, ids_ref, lists_ref):
    member = lax.axis_index("frames")
    rows, columns = ids_ref.shape
    lanes = lists_ref.shape[1] // members
    shape = (rows, members * lanes)
    lane = lax.broadcasted_iota(jnp.int32, shape, 1)
    distance = lane // lanes
    within = lane - distance * lanes
    shard = jnp.bitwise_xor(distance, member)
    low = shard * tiles_here
    count = jnp.broadcast_to(ids_ref[:, columns - 1 : columns], shape)
    taken = jnp.zeros(shape, jnp.int32)
    lists = jnp.zeros(shape, jnp.int32)
    for at in range(columns - 1):
        entry = jnp.broadcast_to(ids_ref[:, at : at + 1], shape) - low
        here = (entry >= 0) & (entry < tiles_here) & (at < count)
        lists = jnp.where(here & (within == taken), entry, lists)
        taken = taken + here.astype(jnp.int32)
    lists_ref[...] = jnp.where(within == lanes - 1, taken, lists)


def route_kernel(own_ref, near_ref, out_ref):
    quarter_tiles = out_ref.shape[0] // 4
    piece = lax.axis_index("medoids")
    row = 0
    for at in (piece, jnp.bitwise_xor(piece, 2)):
        for ref in (own_ref, near_ref):
            for tile in range(quarter_tiles):
                out_ref[row : row + 1, :] = ref[pl.ds(at * quarter_tiles + tile, 1), :]
                row += 1


def stack_kernel(*refs):
    out_ref = refs[-1]
    rows = out_ref.shape[1]
    for index, ref in enumerate(refs[:-1]):
        out_ref[index] = ref[rows:, :]


def norms_kernel(scale, *refs):
    norms_ref = refs[-1]
    row = 0
    for ref in refs[:-1]:
        for tile in range(ref.shape[0] // TILE):
            rows = ref[tile * TILE : (tile + 1) * TILE, :].astype(jnp.float32)
            norms_ref[row : row + 1, :] = scale * column_of(rows * rows)
            row += 1


def search(
    tiles, slots, first_tile, quarter_tiles, tiles_here, lists, rows_ref, norms_ref,
    frames_ref, one_ref, two_ref, table_ref,
):
    lanes, listed = lists
    dummy = len(slots) * tiles_here
    shift = 16

    def place_of(index):
        zslot = index // quarter_tiles
        return zslot, index - zslot * quarter_tiles

    def ends_of(index):
        zslot, tile = place_of(index)
        ends, number = [], jnp.int32(0)
        for slot in slots:
            number = number + listed(zslot, slot, tile, lanes - 1)
            ends.append(number)
        return ends

    def blocks_of(at, written):
        blocks = (ends_of(first_tile + at)[-1] + unroll - 1) // unroll

        def put(block, _):
            table_ref[written + block] = (block << shift) + at
            return 0

        lax.fori_loop(0, blocks, put, 0)
        return written + blocks

    written = lax.fori_loop(0, tiles, blocks_of, jnp.int32(0))
    for extra in range(together - 1):
        table_ref[written + extra] = jnp.int32(1 << (shift + 8))
    size = tiles * TILE
    one_ref[0:size, :] = jnp.full((size, TILE), big_value, jnp.float32)
    two_ref[0:size, :] = jnp.full((size, TILE), big_value, jnp.float32)

    def step(at_step, _):
        results = []
        for member in range(together):
            code = table_ref[at_step * together + member]
            at = jnp.bitwise_and(code, (1 << shift) - 1)
            block = code >> shift
            index = first_tile + at
            zslot, tile = place_of(index)
            ends = ends_of(index)
            picked, picked_norm = [], []
            for lane in range(unroll):
                place = block * unroll + lane
                live = place < ends[-1]
                slot, start = jnp.int32(0), jnp.int32(0)
                for number in range(1, len(slots)):
                    beyond = place >= ends[number - 1]
                    slot = jnp.where(beyond, number, slot)
                    start = jnp.where(beyond, ends[number - 1], start)
                place = jnp.where(live, place - start, 0)
                entry = listed(zslot, slots[0] + slot, tile, place) + slot * tiles_here
                row = jnp.where(live, entry, 0) * TILE
                picked.append(rows_ref[pl.ds(pl.multiple_of(row, TILE), TILE), :])
                picked_norm.append(norms_ref[pl.ds(jnp.where(live, entry, dummy), 1), :])
            inner = lax.dot_general(
                frames_ref[pl.ds(pl.multiple_of(index * TILE, TILE), TILE), :],
                jnp.concatenate(picked, axis=0),
                (((1,), (1,)), ((), ())),
                preferred_element_type=jnp.float32,
            )
            results.append((at, picked_norm, inner))
        for at, picked_norm, inner in results:
            rows = pl.ds(pl.multiple_of(at * TILE, TILE), TILE)
            one, two = one_ref[rows, :], two_ref[rows, :]
            for lane in range(unroll):
                part = picked_norm[lane] - inner[:, lane * TILE : (lane + 1) * TILE]
                two = jnp.minimum(two, jnp.maximum(one, part))
                one = jnp.minimum(one, part)
            one_ref[rows, :] = one
            two_ref[rows, :] = two
        return 0

    lax.fori_loop(0, (written + together - 1) // together, step, 0)


def lists_by_distance(lists_ref, quarter_tiles):
    lanes = lists_ref.shape[2] // lists_ref.shape[0]

    def listed(zslot, slot, tile, place):
        return lists_ref[zslot, slot * quarter_tiles + tile, zslot * lanes + place]

    return lanes, listed


def store_rows(tiles, out_ref, one_buf, two_buf):
    for index in range(tiles):
        rows = pl.ds(index * TILE, TILE)
        one, two = row_pair(one_buf[rows, :], two_buf[rows, :])
        out_ref[0, index : index + 1, :] = one
        out_ref[1, index : index + 1, :] = two


def start_all(pairs, sems):
    copies = [
        pltpu.make_async_copy(source, target, sems.at[index])
        for index, (source, target) in enumerate(pairs)
    ]
    for copy in copies:
        copy.start()
    return copies


def own_kernel(
    members, own_listed, near_listed, norms_own, norms_near, own_group, near_group, own_frames,
    out_ref, lists_ref, rows_buf, norms_buf, one_buf, two_buf, table_ref, sems,
):
    tile_rows = own_group.shape[0]
    tiles_here = tile_rows // TILE
    quarter_tiles = own_frames.shape[0] // TILE
    first = lax.axis_index("medoids") * quarter_tiles
    copies = start_all(
        (
            (own_group, rows_buf.at[pl.ds(0, tile_rows)]),
            (near_group, rows_buf.at[pl.ds(tile_rows, tile_rows)]),
            (own_listed, lists_ref.at[0]),
            (near_listed, lists_ref.at[1]),
        ),
        sems,
    )
    norms_buf[pl.ds(0, tiles_here), :] = norms_own[...]
    norms_buf[pl.ds(tiles_here, tiles_here), :] = norms_near[...]
    norms_buf[pl.ds(2 * tiles_here, 1), :] = jnp.full((1, TILE), big_value, jnp.float32)
    for copy in copies:
        copy.wait()

    def listed(zslot, slot, tile, place):
        return lists_ref[slot, first + tile, place]

    search(
        quarter_tiles, (0, 1), 0, quarter_tiles, tiles_here, (TILE // members, listed), rows_buf,
        norms_buf, own_frames, one_buf, two_buf, table_ref,
    )
    store_rows(quarter_tiles, out_ref, one_buf, two_buf)


def near_kernel(
    lists_1, lists_2, norms_own, norms_near, own_group, near_group,
    frames_1, frames_2,
    out_ref, lists_ref, rows_buf, frames_buf, norms_buf, one_buf, two_buf, table_ref, sems,
):
    tile_rows = own_group.shape[0]
    tiles_here = tile_rows // TILE
    quarter = frames_1.shape[0]
    quarter_tiles = quarter // TILE
    copies = start_all(
        (
            (own_group, rows_buf.at[pl.ds(0, tile_rows)]),
            (near_group, rows_buf.at[pl.ds(tile_rows, tile_rows)]),
            (frames_1, frames_buf.at[pl.ds(quarter, quarter)]),
            (frames_2, frames_buf.at[pl.ds(2 * quarter, quarter)]),
            (lists_1.at[pl.ds(0, 2 * quarter_tiles)], lists_ref.at[1]),
            (lists_2.at[pl.ds(0, 2 * quarter_tiles)], lists_ref.at[2]),
        ),
        sems,
    )
    norms_buf[pl.ds(0, tiles_here), :] = norms_own[...]
    norms_buf[pl.ds(tiles_here, tiles_here), :] = norms_near[...]
    norms_buf[pl.ds(2 * tiles_here, 1), :] = jnp.full((1, TILE), big_value, jnp.float32)
    for copy in copies:
        copy.wait()
    search(
        2 * quarter_tiles, (0, 1), quarter_tiles, quarter_tiles, tiles_here,
        lists_by_distance(lists_ref, quarter_tiles), rows_buf, norms_buf,
        frames_buf, one_buf, two_buf, table_ref,
    )
    store_rows(2 * quarter_tiles, out_ref, one_buf, two_buf)


def far_kernel(
    near_lists, far_lists, norms_own, norms_near, norms_far, before_own, before_near, frame_norms,
    own_group, near_group, far_a, far_b, far_c, last_a, last_b, last_c,
    own_frames, frames_1, frames_2, frames_3a, frames_3b,
    out_ref, lists_ref, rows_buf, frames_buf, norms_buf, one_buf, two_buf, table_ref, sems,
):
    tile_rows = own_group.shape[0]
    tiles_here = tile_rows // TILE
    groups = 2 + norms_far.shape[0]
    quarter = own_frames.shape[0]
    quarter_tiles = quarter // TILE
    width = own_frames.shape[1]
    members = frames_buf.shape[0] // quarter
    member = lax.axis_index("frames")
    slab = lax.axis_index("slab")
    side = far_a.shape[0]
    middle = far_b.shape[0]
    near_side = slab * (tile_rows - side)
    other_side = (1 - slab) * (tile_rows - side)

    copies = []

    def bring(source, target, start, rows):
        copies.append(
            pltpu.make_async_copy(
                source, target.at[pl.ds(pl.multiple_of(start, TILE), rows)], sems.at[len(copies)]
            )
        )

    for slot, (first_piece, second_piece, third_piece) in (
        (2, (far_a, far_b, far_c)),
        (3, (last_a, last_b, last_c)),
    ):
        bring(first_piece, rows_buf, slot * tile_rows + near_side, side)
        bring(second_piece, rows_buf, slot * tile_rows + side, middle)
        bring(third_piece, rows_buf, slot * tile_rows + other_side, side)
    bring(own_frames, frames_buf, 0, quarter)
    bring(frames_1, frames_buf, quarter, quarter)
    bring(frames_2, frames_buf, 2 * quarter, quarter)
    pair_rows = 2 * quarter_tiles
    for index in range(members):
        target = lists_ref.at[index, pl.ds(pair_rows, pair_rows)]
        copies.append(pltpu.make_async_copy(far_lists.at[index], target, sems.at[len(copies)]))
    target = lists_ref.at[members - 1, pl.ds(0, pair_rows)]
    copies.append(
        pltpu.make_async_copy(near_lists.at[pl.ds(0, pair_rows)], target, sems.at[len(copies)])
    )
    early = len(copies)
    bring(own_group, rows_buf, 0, tile_rows)
    bring(near_group, rows_buf, tile_rows, tile_rows)
    for copy in copies[:early]:
        copy.start()
    inner_member = jnp.logical_and(member > 0, member < members - 1)
    last_sem = sems.at[len(copies)]
    last_target = frames_buf.at[pl.ds(3 * quarter, quarter)]

    @pl.when(inner_member)
    def _():
        pltpu.make_async_copy(frames_3a, last_target, last_sem).start()

    @pl.when(jnp.logical_not(inner_member))
    def _():
        pltpu.make_async_copy(frames_3b, last_target, last_sem).start()

    for copy in copies[early:]:
        copy.start()

    dummy = groups * tiles_here
    for slot, norms in enumerate((norms_own, norms_near, norms_far.at[0], norms_far.at[1])):
        norms_buf[pl.ds(slot * tiles_here, tiles_here), :] = norms[...]
    norms_buf[pl.ds(dummy, 1), :] = jnp.full((1, TILE), big_value, jnp.float32)
    for copy in copies[:early]:
        copy.wait()

    def finish(index, at, before_one, before_two, frame_norm):
        rows = pl.ds(at * TILE, TILE)
        one, two = row_pair(one_buf[rows, :], two_buf[rows, :])
        if before_one is not None:
            one, two = fold_two(one, two, before_one, before_two)
        block_of = jnp.bitwise_xor(member, index // quarter_tiles)
        row = block_of * quarter_tiles + index % quarter_tiles
        out_ref[0, pl.ds(row, 1), :] = (frame_norm + 2.0 * one) / width
        out_ref[1, pl.ds(row, 1), :] = (frame_norm + 2.0 * two) / width

    early_tiles = 3 * quarter_tiles
    lists = lists_by_distance(lists_ref, quarter_tiles)
    search(
        early_tiles, (2, 3), 0, quarter_tiles, tiles_here, lists,
        rows_buf.at[pl.ds(2 * tile_rows, 2 * tile_rows)],
        norms_buf.at[pl.ds(2 * tiles_here, 2 * tiles_here + 8)],
        frames_buf, one_buf, two_buf, table_ref,
    )
    for index in range(early_tiles):
        before, at = before_own, index
        if index >= quarter_tiles:
            before, at = before_near, index - quarter_tiles
        finish(
            index, index, before[0, at : at + 1, :], before[1, at : at + 1, :],
            frame_norms[index : index + 1, :],
        )
    pltpu.make_async_copy(frames_3a, last_target, last_sem).wait()
    for copy in copies[early:]:
        copy.wait()
    search(
        quarter_tiles, tuple(range(groups)), early_tiles, quarter_tiles, tiles_here, lists,
        rows_buf, norms_buf, frames_buf, one_buf, two_buf, table_ref,
    )
    for tile in range(quarter_tiles):
        rows = frames_buf[pl.ds((early_tiles + tile) * TILE, TILE), :].astype(jnp.float32)
        finish(early_tiles + tile, tile, None, None, column_of(rows * rows))


def pick_kernel(plan_ref, part_0, part_1, part_2, part_3, first_ref, second_ref, every):
    member = lax.axis_index("frames")
    piece = lax.axis_index("medoids")
    blocks = first_ref.shape[0]
    parts = (part_0, part_1, part_2, part_3)
    quarter_tiles = blocks // len(parts)
    rows = part_0.shape[1]
    for slot, part in enumerate(parts):
        every[:, slot * rows : (slot + 1) * rows, :] = part[...]
    for place in range(blocks):
        tile = plan_ref[member * blocks + place]
        block_of = tile // blocks
        inside = tile - block_of * blocks
        part = inside // quarter_tiles
        row = jnp.bitwise_xor(part, piece) * rows + block_of * quarter_tiles + (inside - part * quarter_tiles)
        first_ref[pl.ds(place, 1), :] = every[0, pl.ds(row, 1), :]
        second_ref[pl.ds(place, 1), :] = every[1, pl.ds(row, 1), :]


def exchanged(number, distance):
    return [(at, at ^ distance) for at in range(number)]


def gathered_frames(frames, medoids, tile_ids, tile_counts, plan):
    width = frames.shape[1]
    blocks = frames.shape[0] // TILE
    members = lax.axis_size("frames")
    groups = lax.axis_size("medoids")
    rows = medoids[0]
    tile_rows = rows.shape[0]
    quarter_tiles = blocks // groups
    quarter = quarter_tiles * TILE
    side = tile_rows // TILE // 3 * TILE

    hbm = pl.BlockSpec(memory_space=pl.ANY)
    scalar = pl.BlockSpec(memory_space=pltpu.SMEM)
    vector = pl.BlockSpec(memory_space=pltpu.VMEM)
    small = pltpu.CompilerParams(vmem_limit_bytes=small_vmem)
    large = pltpu.CompilerParams(vmem_limit_bytes=large_vmem)
    mine, edge = pl.pallas_call(
        cut_first_kernel,
        out_shape=(
            jax.ShapeDtypeStruct((quarter, width), frames.dtype),
            jax.ShapeDtypeStruct((side, width), rows.dtype),
        ),
        in_specs=[hbm, hbm],
        out_specs=(vector, vector),
        scratch_shapes=[pltpu.SemaphoreType.DMA((2,))],
        compiler_params=pltpu.CompilerParams(vmem_limit_bytes=whole_vmem),
        name="cut_first",
    )(frames, rows)
    inside_rows = pl.pallas_call(
        functools.partial(cut_middle_kernel, side),
        out_shape=jax.ShapeDtypeStruct((tile_rows - 2 * side, width), rows.dtype),
        in_specs=[hbm],
        out_specs=vector,
        scratch_shapes=[pltpu.SemaphoreType.DMA],
        compiler_params=small,
        name="cut_middle",
    )(rows)
    frames_2 = lax.ppermute(mine, "frames", exchanged(members, 2))
    frames_1 = lax.ppermute(mine, "frames", exchanged(members, 1))
    frames_3a = lax.ppermute(mine, "frames", [(1, 2), (2, 1)])
    frames_3b = lax.ppermute(frames_2, "frames", [(2, 3), (1, 0)])

    far_a = lax.ppermute(edge, "medoids", exchanged(groups, 2))
    far_b = lax.ppermute(inside_rows, "medoids", exchanged(groups, 2))
    far_c = lax.ppermute(far_a, "slab", exchanged(2, 1))
    near_group = lax.ppermute(rows, "medoids", exchanged(groups, 1))
    last_a = lax.ppermute(far_a, "medoids", exchanged(groups, 1))
    last_b = lax.ppermute(far_b, "medoids", exchanged(groups, 1))
    last_c = lax.ppermute(far_c, "medoids", exchanged(groups, 1))

    tiles_here = tile_rows // TILE
    listed = pl.pallas_call(
        functools.partial(split_kernel, members, tiles_here),
        out_shape=jax.ShapeDtypeStruct((blocks, TILE), jnp.int32),
        in_specs=[vector],
        out_specs=vector,
        compiler_params=small,
        name="split",
    )(jnp.concatenate([tile_ids[0], tile_counts[0][:, None]], axis=1))
    near_listed = lax.ppermute(listed, "medoids", exchanged(groups, 1))
    routed = pl.pallas_call(
        route_kernel,
        out_shape=jax.ShapeDtypeStruct((4 * quarter_tiles, TILE), jnp.int32),
        in_specs=[vector] * 2,
        out_specs=vector,
        compiler_params=small,
        name="route",
    )(listed, near_listed)
    near_lists = [lax.ppermute(routed, "frames", exchanged(members, at)) for at in (1, 2, 3)]
    far_lists = pl.pallas_call(
        stack_kernel,
        out_shape=jax.ShapeDtypeStruct((members, 2 * quarter_tiles, TILE), jnp.int32),
        in_specs=[vector] * 4,
        out_specs=vector,
        compiler_params=small,
        name="stack_far",
    )(routed, *near_lists)
    far_lists = lax.ppermute(far_lists, "medoids", exchanged(groups, 2))
    norms = pl.pallas_call(
        functools.partial(norms_kernel, 0.5),
        out_shape=jax.ShapeDtypeStruct((tiles_here, TILE), jnp.float32),
        in_specs=[vector],
        out_specs=vector,
        compiler_params=small,
        name="medoid_norms",
    )(rows)
    norm_near = lax.ppermute(norms, "medoids", exchanged(groups, 1))
    norm_pair = jnp.stack([norms, norm_near])
    norm_far = lax.ppermute(norm_pair, "medoids", exchanged(groups, 2))
    frame_norms = pl.pallas_call(
        functools.partial(norms_kernel, 1.0),
        out_shape=jax.ShapeDtypeStruct((3 * quarter_tiles, TILE), jnp.float32),
        in_specs=[vector] * 3,
        out_specs=vector,
        compiler_params=small,
        name="frame_norms",
    )(mine, frames_1, frames_2)

    total_tiles = members * quarter_tiles
    early_tiles = 3 * quarter_tiles
    table_size = early_tiles * (groups * tile_ids.shape[2] // unroll + 1) + together
    before_own = pl.pallas_call(
        functools.partial(own_kernel, members),
        out_shape=jax.ShapeDtypeStruct((2, quarter_tiles, TILE), jnp.float32),
        in_specs=[hbm] * 2 + [vector] * 2 + [hbm] * 2 + [vector],
        out_specs=vector,
        scratch_shapes=[
            pltpu.SMEM((2, blocks, TILE), jnp.int32),
            pltpu.VMEM((2 * tile_rows, width), jnp.bfloat16),
            pltpu.VMEM((2 * tiles_here + 8, TILE), jnp.float32),
            pltpu.VMEM((quarter, TILE), jnp.float32),
            pltpu.VMEM((quarter, TILE), jnp.float32),
            pltpu.SMEM((table_size,), jnp.int32),
            pltpu.SemaphoreType.DMA((4,)),
        ],
        compiler_params=large,
        name="own_search",
    )(listed, near_listed, norms, norm_near, rows, near_group, mine)
    before_near = pl.pallas_call(
        near_kernel,
        out_shape=jax.ShapeDtypeStruct((2, 2 * quarter_tiles, TILE), jnp.float32),
        in_specs=[hbm] * 2 + [vector] * 2 + [hbm] * 4,
        out_specs=vector,
        scratch_shapes=[
            pltpu.SMEM((members, 2 * quarter_tiles, TILE), jnp.int32),
            pltpu.VMEM((2 * tile_rows, width), jnp.bfloat16),
            pltpu.VMEM((3 * quarter, width), jnp.bfloat16),
            pltpu.VMEM((2 * tiles_here + 8, TILE), jnp.float32),
            pltpu.VMEM((2 * quarter, TILE), jnp.float32),
            pltpu.VMEM((2 * quarter, TILE), jnp.float32),
            pltpu.SMEM((table_size,), jnp.int32),
            pltpu.SemaphoreType.DMA((8,)),
        ],
        compiler_params=large,
        name="near_search",
    )(*near_lists[:2], norms, norm_near, rows, near_group, frames_1, frames_2)
    found = pl.pallas_call(
        far_kernel,
        out_shape=jax.ShapeDtypeStruct((2, total_tiles, TILE), jnp.float32),
        in_specs=[hbm] * 2 + [vector] * 6 + [hbm] * 13,
        out_specs=vector,
        scratch_shapes=[
            pltpu.SMEM((members, groups * quarter_tiles, TILE), jnp.int32),
            pltpu.VMEM((groups * tile_rows, width), jnp.bfloat16),
            pltpu.VMEM((members * quarter, width), jnp.bfloat16),
            pltpu.VMEM((groups * tiles_here + 8, TILE), jnp.float32),
            pltpu.VMEM((3 * quarter, TILE), jnp.float32),
            pltpu.VMEM((3 * quarter, TILE), jnp.float32),
            pltpu.SMEM((table_size,), jnp.int32),
            pltpu.SemaphoreType.DMA((20,)),
        ],
        compiler_params=large,
        name="far_search",
    )(
        near_lists[2], far_lists, norms, norm_near, norm_far, before_own, before_near, frame_norms, rows, near_group,
        far_a, far_b, far_c, last_a, last_b, last_c, mine, frames_1, frames_2, frames_3a, frames_3b,
    )

    one, two = found[0], found[1]
    for at in (1, 2, 3):
        other = lax.ppermute(found, "frames", exchanged(members, at))
        one, two = fold_two(one, two, other[0], other[1])
    merged = jnp.stack([one, two])
    parts = [merged] + [lax.ppermute(merged, "medoids", exchanged(groups, at)) for at in (1, 2, 3)]
    first, second = pl.pallas_call(
        pick_kernel,
        out_shape=(jax.ShapeDtypeStruct((blocks, TILE), jnp.float32),) * 2,
        in_specs=[scalar] + [vector] * 4,
        out_specs=(vector, vector),
        scratch_shapes=[pltpu.VMEM((2, groups * members * quarter_tiles, TILE), jnp.float32)],
        compiler_params=small,
        name="pick",
    )(plan, *parts)
    return (first.reshape(-1), second.reshape(-1))


def solution(mesh):
    placed = (
        P(("slab", "frames"), None),
        P("medoids", "frames", None),
        P("medoids", ("slab", "frames"), None),
        P("medoids", ("slab", "frames")),
        P("slab"),
    )

    def per_device(frames, medoids, tile_ids, tile_counts, plan):
        blocks = frames.shape[0] // TILE
        quarters = mesh.shape["frames"] == 4 and mesh.shape["medoids"] == 4 and mesh.shape["slab"] == 2
        if quarters and blocks % 4 == 0 and medoids.shape[1] // TILE >= 3:
            return gathered_frames(frames, medoids, tile_ids, tile_counts, plan)
        return gathered_medoids(frames, medoids, tile_ids, tile_counts, plan)

    return jax.shard_map(
        per_device,
        mesh=mesh,
        in_specs=placed,
        out_specs=(P(("slab", "frames")), P(("slab", "frames"))),
        check_vma=False,
    )
```

```python
import functools

import jax
import jax.numpy as jnp
from jax import lax
from jax.experimental import pallas as pl
from jax.experimental.pallas import tpu as pltpu
from jax.sharding import PartitionSpec as P


TILE = 128
frame_axis, group_axis, slab_axis = "frames", "medoids", "slab"


big_value = 1e30
per_block = 8
unroll = 2
together = 8
small_vmem = 8 << 20
large_vmem = 24 << 20
whole_vmem = 125 << 19


def fold_two(left_one, left_two, right_one, right_two):
    first = jnp.minimum(left_one, right_one)
    second = jnp.minimum(jnp.maximum(left_one, right_one), jnp.minimum(left_two, right_two))
    return (first, second)


def tile_pass(frame_tile, ids, count, group_rows, group_norm):
    width = frame_tile.shape[1]
    rows_tile = frame_tile.shape[0]
    frame_norm = jnp.sum(jnp.square(frame_tile.astype(jnp.float32)), axis=1)

    def step(block, carry):
        start = (block * per_block).astype(jnp.int32)
        chosen = lax.dynamic_slice_in_dim(ids, start, per_block)
        live = start + jnp.arange(per_block, dtype=jnp.int32) < count
        rows = group_rows[chosen].reshape(per_block * rows_tile, width)
        norms = group_norm[chosen].reshape(per_block * rows_tile)
        inner = lax.dot_general(
            frame_tile, rows, (((1,), (1,)), ((), ())), preferred_element_type=jnp.float32
        )
        dist = (frame_norm[:, None] + norms[None, :] - 2.0 * inner) / width
        keep = jnp.repeat(live, rows_tile)
        dist = jnp.where(keep[None, :], dist, jnp.float32(big_value))
        lowest = -lax.top_k(-dist, 2)[0]
        return fold_two(carry[0], carry[1], lowest[:, 0], lowest[:, 1])

    start_pair = (
        jnp.full((rows_tile,), big_value, jnp.float32),
        jnp.full((rows_tile,), big_value, jnp.float32),
    )
    blocks = (count + per_block - 1) // per_block
    return lax.fori_loop(0, blocks, step, start_pair)


def all_tiles(tiles, ids, counts, group_rows, group_norm):
    number = tiles.shape[0]

    def one_tile(index, carry):
        found_one, found_two = tile_pass(
            tiles[index], ids[index], counts[index], group_rows, group_norm
        )
        return (carry[0].at[index].set(found_one), carry[1].at[index].set(found_two))

    empty = jnp.zeros((number, TILE), jnp.float32)
    return lax.fori_loop(0, number, one_tile, (empty, empty))


def across_groups(first, second):
    every_one, every_two = (
        lax.all_gather(first[None], group_axis, axis=0, tiled=True),
        lax.all_gather(second[None], group_axis, axis=0, tiled=True),
    )
    best_one, best_two = (every_one[0], every_two[0])
    for group in range(1, every_one.shape[0]):
        best_one, best_two = fold_two(best_one, best_two, every_one[group], every_two[group])
    return (best_one, best_two)


def gathered_medoids(frames, medoids, tile_ids, tile_counts, plan):
    width = frames.shape[1]
    blocks = frames.shape[0] // TILE
    members = lax.axis_size(frame_axis)
    member = lax.axis_index(frame_axis)
    capacity = (blocks + members - 1) // members
    group = lax.all_gather(medoids[0], frame_axis, axis=0, tiled=True)
    group_tiles = group.shape[0] // TILE
    group_rows = group.reshape(group_tiles, TILE, width)
    group_norm = jnp.sum(jnp.square(group.astype(jnp.float32)), axis=1).reshape(group_tiles, TILE)
    total = plan.shape[0]
    position = jnp.zeros((total,), jnp.int32).at[plan].set(jnp.arange(total, dtype=jnp.int32))
    target = (position // blocks).reshape(members, blocks)
    matching = target[:, :, None] == target[:, None, :]
    earlier = jnp.arange(blocks)[None, :] < jnp.arange(blocks)[:, None]
    slot_table = jnp.sum(jnp.logical_and(matching, earlier[None]), axis=2)
    my_target = lax.dynamic_index_in_dim(target, member, 0, keepdims=False)
    my_slot = lax.dynamic_index_in_dim(slot_table, member, 0, keepdims=False)
    arriving = lax.dynamic_slice_in_dim(plan, member * blocks, blocks)
    sender = arriving // blocks
    sender_slot = slot_table.reshape(-1)[arriving]
    tiles = frames.reshape(blocks, TILE, width)
    outgoing_tiles = (
        jnp.zeros((members, capacity, TILE, width), frames.dtype).at[my_target, my_slot].set(tiles)
    )
    outgoing_ids = (
        jnp.zeros((members, capacity, tile_ids.shape[2]), jnp.int32)
        .at[my_target, my_slot]
        .set(tile_ids[0])
    )
    outgoing_counts = (
        jnp.zeros((members, capacity), jnp.int32).at[my_target, my_slot].set(tile_counts[0])
    )
    incoming_tiles, incoming_ids, incoming_counts = (
        lax.all_to_all(outgoing_tiles, frame_axis, split_axis=0, concat_axis=0, tiled=True),
        lax.all_to_all(outgoing_ids, frame_axis, split_axis=0, concat_axis=0, tiled=True),
        lax.all_to_all(outgoing_counts, frame_axis, split_axis=0, concat_axis=0, tiled=True),
    )
    placed_tiles = incoming_tiles[sender, sender_slot]
    placed_ids = incoming_ids[sender, sender_slot]
    placed_counts = incoming_counts[sender, sender_slot]
    first, second = all_tiles(placed_tiles, placed_ids, placed_counts, group_rows, group_norm)
    first, second = across_groups(first, second)
    return (first.reshape(-1), second.reshape(-1))


def column_of(squares):
    total = squares[:, 0:TILE]
    for at_lane in range(TILE, squares.shape[1], TILE):
        total = total + squares[:, at_lane : at_lane + TILE]
    return jnp.sum(total.T, axis=0, keepdims=True)


def row_pair(one, two):
    one, two = one.T, two.T
    rows = one.shape[0]
    while rows > 8:
        half = rows // 2
        one, two = fold_two(one[:half], two[:half], one[half:], two[half:])
        rows = half
    for shift in (4, 2, 1):
        one, two = fold_two(one, two, pltpu.roll(one, shift, 0), pltpu.roll(two, shift, 0))
    return one[0:1], two[0:1]


def cut_first_kernel(frames_ref, group_ref, mine_ref, edge_ref, sems):
    quarter, side = mine_ref.shape[0], edge_ref.shape[0]
    start = pl.multiple_of(lax.axis_index(group_axis) * quarter, TILE)
    end = pl.multiple_of(lax.axis_index(slab_axis) * (group_ref.shape[0] - side), TILE)
    copies = start_all(
        (
            (frames_ref.at[pl.ds(start, quarter)], mine_ref),
            (group_ref.at[pl.ds(end, side)], edge_ref),
        ),
        sems,
    )
    for copy in copies:
        copy.wait()


def cut_middle_kernel(side, group_ref, middle_ref, sem):
    copy = pltpu.make_async_copy(group_ref.at[pl.ds(side, middle_ref.shape[0])], middle_ref, sem)
    copy.start()
    copy.wait()


def split_kernel(members, tiles_here, ids_ref, lists_ref):
    member = lax.axis_index(frame_axis)
    rows, columns = ids_ref.shape
    lanes = lists_ref.shape[1] // members
    shape = (rows, members * lanes)
    lane = lax.broadcasted_iota(jnp.int32, shape, 1)
    distance = lane // lanes
    within = lane - distance * lanes
    shard = jnp.bitwise_xor(distance, member)
    low = shard * tiles_here
    count = jnp.broadcast_to(ids_ref[:, columns - 1 : columns], shape)
    taken = jnp.zeros(shape, jnp.int32)
    lists = jnp.zeros(shape, jnp.int32)
    for at in range(columns - 1):
        entry = jnp.broadcast_to(ids_ref[:, at : at + 1], shape) - low
        here = (entry >= 0) & (entry < tiles_here) & (at < count)
        lists = jnp.where(here & (within == taken), entry, lists)
        taken = taken + here.astype(jnp.int32)
    lists_ref[...] = jnp.where(within == lanes - 1, taken, lists)


def route_kernel(own_ref, near_ref, out_ref):
    quarter_tiles = out_ref.shape[0] // 4
    piece = lax.axis_index(group_axis)
    row = 0
    for at in (piece, jnp.bitwise_xor(piece, 2)):
        for ref in (own_ref, near_ref):
            for tile in range(quarter_tiles):
                out_ref[row : row + 1, :] = ref[pl.ds(at * quarter_tiles + tile, 1), :]
                row += 1


def stack_kernel(*refs):
    out_ref = refs[-1]
    rows = out_ref.shape[1]
    for index, ref in enumerate(refs[:-1]):
        out_ref[index] = ref[rows:, :]


def norms_kernel(scale, *refs):
    norms_ref = refs[-1]
    row = 0
    for ref in refs[:-1]:
        for tile in range(ref.shape[0] // TILE):
            rows = ref[tile * TILE : (tile + 1) * TILE, :].astype(jnp.float32)
            norms_ref[row : row + 1, :] = scale * column_of(rows * rows)
            row += 1


def search(
    tiles, slots, first_tile, quarter_tiles, tiles_here, lists, rows_ref, norms_ref,
    frames_ref, one_ref, two_ref, table_ref,
):
    lanes, listed = lists
    dummy = len(slots) * tiles_here
    shift = 16

    def place_of(index):
        zslot = index // quarter_tiles
        return zslot, index - zslot * quarter_tiles

    def ends_of(index):
        zslot, tile = place_of(index)
        ends, number = [], jnp.int32(0)
        for slot in slots:
            number = number + listed(zslot, slot, tile, lanes - 1)
            ends.append(number)
        return ends

    def blocks_of(at, written):
        blocks = (ends_of(first_tile + at)[-1] + unroll - 1) // unroll

        def put(block, _):
            table_ref[written + block] = (block << shift) + at
            return 0

        lax.fori_loop(0, blocks, put, 0)
        return written + blocks

    written = lax.fori_loop(0, tiles, blocks_of, jnp.int32(0))
    for extra in range(together - 1):
        table_ref[written + extra] = jnp.int32(1 << (shift + 8))
    size = tiles * TILE
    one_ref[0:size, :] = jnp.full((size, TILE), big_value, jnp.float32)
    two_ref[0:size, :] = jnp.full((size, TILE), big_value, jnp.float32)

    def step(at_step, _):
        results = []
        for member in range(together):
            code = table_ref[at_step * together + member]
            at = jnp.bitwise_and(code, (1 << shift) - 1)
            block = code >> shift
            index = first_tile + at
            zslot, tile = place_of(index)
            ends = ends_of(index)
            picked, picked_norm = [], []
            for lane in range(unroll):
                place = block * unroll + lane
                live = place < ends[-1]
                slot, start = jnp.int32(0), jnp.int32(0)
                for number in range(1, len(slots)):
                    beyond = place >= ends[number - 1]
                    slot = jnp.where(beyond, number, slot)
                    start = jnp.where(beyond, ends[number - 1], start)
                place = jnp.where(live, place - start, 0)
                entry = listed(zslot, slots[0] + slot, tile, place) + slot * tiles_here
                row = jnp.where(live, entry, 0) * TILE
                picked.append(rows_ref[pl.ds(pl.multiple_of(row, TILE), TILE), :])
                picked_norm.append(norms_ref[pl.ds(jnp.where(live, entry, dummy), 1), :])
            inner = lax.dot_general(
                frames_ref[pl.ds(pl.multiple_of(index * TILE, TILE), TILE), :],
                jnp.concatenate(picked, axis=0),
                (((1,), (1,)), ((), ())),
                preferred_element_type=jnp.float32,
            )
            results.append((at, picked_norm, inner))
        for at, picked_norm, inner in results:
            rows = pl.ds(pl.multiple_of(at * TILE, TILE), TILE)
            one, two = one_ref[rows, :], two_ref[rows, :]
            for lane in range(unroll):
                part = picked_norm[lane] - inner[:, lane * TILE : (lane + 1) * TILE]
                two = jnp.minimum(two, jnp.maximum(one, part))
                one = jnp.minimum(one, part)
            one_ref[rows, :] = one
            two_ref[rows, :] = two
        return 0

    lax.fori_loop(0, (written + together - 1) // together, step, 0)


def lists_by_distance(lists_ref, quarter_tiles):
    lanes = lists_ref.shape[2] // lists_ref.shape[0]

    def listed(zslot, slot, tile, place):
        return lists_ref[zslot, slot * quarter_tiles + tile, zslot * lanes + place]

    return lanes, listed


def store_rows(tiles, out_ref, one_buf, two_buf):
    for index in range(tiles):
        rows = pl.ds(index * TILE, TILE)
        one, two = row_pair(one_buf[rows, :], two_buf[rows, :])
        out_ref[0, index : index + 1, :] = one
        out_ref[1, index : index + 1, :] = two


def start_all(pairs, sems):
    copies = [
        pltpu.make_async_copy(source, target, sems.at[index])
        for index, (source, target) in enumerate(pairs)
    ]
    for copy in copies:
        copy.start()
    return copies


def own_kernel(
    members, own_listed, near_listed, norms_own, norms_near, own_group, near_group, own_frames,
    out_ref, lists_ref, rows_buf, norms_buf, one_buf, two_buf, table_ref, sems,
):
    tile_rows = own_group.shape[0]
    tiles_here = tile_rows // TILE
    quarter_tiles = own_frames.shape[0] // TILE
    first = lax.axis_index(group_axis) * quarter_tiles
    copies = start_all(
        (
            (own_group, rows_buf.at[pl.ds(0, tile_rows)]),
            (near_group, rows_buf.at[pl.ds(tile_rows, tile_rows)]),
            (own_listed, lists_ref.at[0]),
            (near_listed, lists_ref.at[1]),
        ),
        sems,
    )
    norms_buf[pl.ds(0, tiles_here), :] = norms_own[...]
    norms_buf[pl.ds(tiles_here, tiles_here), :] = norms_near[...]
    norms_buf[pl.ds(2 * tiles_here, 1), :] = jnp.full((1, TILE), big_value, jnp.float32)
    for copy in copies:
        copy.wait()

    def listed(zslot, slot, tile, place):
        return lists_ref[slot, first + tile, place]

    search(
        quarter_tiles, (0, 1), 0, quarter_tiles, tiles_here, (TILE // members, listed), rows_buf,
        norms_buf, own_frames, one_buf, two_buf, table_ref,
    )
    store_rows(quarter_tiles, out_ref, one_buf, two_buf)


def near_kernel(
    lists_1, lists_2, norms_own, norms_near, own_group, near_group,
    frames_1, frames_2,
    out_ref, lists_ref, rows_buf, frames_buf, norms_buf, one_buf, two_buf, table_ref, sems,
):
    tile_rows = own_group.shape[0]
    tiles_here = tile_rows // TILE
    quarter = frames_1.shape[0]
    quarter_tiles = quarter // TILE
    copies = start_all(
        (
            (own_group, rows_buf.at[pl.ds(0, tile_rows)]),
            (near_group, rows_buf.at[pl.ds(tile_rows, tile_rows)]),
            (frames_1, frames_buf.at[pl.ds(quarter, quarter)]),
            (frames_2, frames_buf.at[pl.ds(2 * quarter, quarter)]),
            (lists_1.at[pl.ds(0, 2 * quarter_tiles)], lists_ref.at[1]),
            (lists_2.at[pl.ds(0, 2 * quarter_tiles)], lists_ref.at[2]),
        ),
        sems,
    )
    norms_buf[pl.ds(0, tiles_here), :] = norms_own[...]
    norms_buf[pl.ds(tiles_here, tiles_here), :] = norms_near[...]
    norms_buf[pl.ds(2 * tiles_here, 1), :] = jnp.full((1, TILE), big_value, jnp.float32)
    for copy in copies:
        copy.wait()
    search(
        2 * quarter_tiles, (0, 1), quarter_tiles, quarter_tiles, tiles_here,
        lists_by_distance(lists_ref, quarter_tiles), rows_buf, norms_buf,
        frames_buf, one_buf, two_buf, table_ref,
    )
    store_rows(2 * quarter_tiles, out_ref, one_buf, two_buf)


def far_kernel(
    near_lists, far_lists, norms_own, norms_near, norms_far, before_own, before_near, frame_norms,
    own_group, near_group, far_a, far_b, far_c, last_a, last_b, last_c,
    own_frames, frames_1, frames_2, frames_3a, frames_3b,
    out_ref, lists_ref, rows_buf, frames_buf, norms_buf, one_buf, two_buf, table_ref, sems,
):
    tile_rows = own_group.shape[0]
    tiles_here = tile_rows // TILE
    groups = 2 + norms_far.shape[0]
    quarter = own_frames.shape[0]
    quarter_tiles = quarter // TILE
    width = own_frames.shape[1]
    members = frames_buf.shape[0] // quarter
    member = lax.axis_index(frame_axis)
    slab = lax.axis_index(slab_axis)
    side = far_a.shape[0]
    middle = far_b.shape[0]
    near_side = slab * (tile_rows - side)
    other_side = (1 - slab) * (tile_rows - side)

    copies = []

    def bring(source, target, start, rows):
        copies.append(
            pltpu.make_async_copy(
                source, target.at[pl.ds(pl.multiple_of(start, TILE), rows)], sems.at[len(copies)]
            )
        )

    for slot, (first_piece, second_piece, third_piece) in (
        (2, (far_a, far_b, far_c)),
        (3, (last_a, last_b, last_c)),
    ):
        bring(first_piece, rows_buf, slot * tile_rows + near_side, side)
        bring(second_piece, rows_buf, slot * tile_rows + side, middle)
        bring(third_piece, rows_buf, slot * tile_rows + other_side, side)
    bring(own_frames, frames_buf, 0, quarter)
    bring(frames_1, frames_buf, quarter, quarter)
    bring(frames_2, frames_buf, 2 * quarter, quarter)
    pair_rows = 2 * quarter_tiles
    for index in range(members):
        target = lists_ref.at[index, pl.ds(pair_rows, pair_rows)]
        copies.append(pltpu.make_async_copy(far_lists.at[index], target, sems.at[len(copies)]))
    target = lists_ref.at[members - 1, pl.ds(0, pair_rows)]
    copies.append(
        pltpu.make_async_copy(near_lists.at[pl.ds(0, pair_rows)], target, sems.at[len(copies)])
    )
    early = len(copies)
    bring(own_group, rows_buf, 0, tile_rows)
    bring(near_group, rows_buf, tile_rows, tile_rows)
    for copy in copies[:early]:
        copy.start()
    inner_member = jnp.logical_and(member > 0, member < members - 1)
    last_sem = sems.at[len(copies)]
    last_target = frames_buf.at[pl.ds(3 * quarter, quarter)]

    @pl.when(inner_member)
    def _():
        pltpu.make_async_copy(frames_3a, last_target, last_sem).start()

    @pl.when(jnp.logical_not(inner_member))
    def _():
        pltpu.make_async_copy(frames_3b, last_target, last_sem).start()

    for copy in copies[early:]:
        copy.start()

    dummy = groups * tiles_here
    for slot, norms in enumerate((norms_own, norms_near, norms_far.at[0], norms_far.at[1])):
        norms_buf[pl.ds(slot * tiles_here, tiles_here), :] = norms[...]
    norms_buf[pl.ds(dummy, 1), :] = jnp.full((1, TILE), big_value, jnp.float32)
    for copy in copies[:early]:
        copy.wait()

    def finish(index, at, before_one, before_two, frame_norm):
        rows = pl.ds(at * TILE, TILE)
        one, two = row_pair(one_buf[rows, :], two_buf[rows, :])
        if before_one is not None:
            one, two = fold_two(one, two, before_one, before_two)
        block_of = jnp.bitwise_xor(member, index // quarter_tiles)
        row = block_of * quarter_tiles + index % quarter_tiles
        out_ref[0, pl.ds(row, 1), :] = (frame_norm + 2.0 * one) / width
        out_ref[1, pl.ds(row, 1), :] = (frame_norm + 2.0 * two) / width

    early_tiles = 3 * quarter_tiles
    lists = lists_by_distance(lists_ref, quarter_tiles)
    search(
        early_tiles, (2, 3), 0, quarter_tiles, tiles_here, lists,
        rows_buf.at[pl.ds(2 * tile_rows, 2 * tile_rows)],
        norms_buf.at[pl.ds(2 * tiles_here, 2 * tiles_here + 8)],
        frames_buf, one_buf, two_buf, table_ref,
    )
    for index in range(early_tiles):
        before, at = before_own, index
        if index >= quarter_tiles:
            before, at = before_near, index - quarter_tiles
        finish(
            index, index, before[0, at : at + 1, :], before[1, at : at + 1, :],
            frame_norms[index : index + 1, :],
        )
    pltpu.make_async_copy(frames_3a, last_target, last_sem).wait()
    for copy in copies[early:]:
        copy.wait()
    search(
        quarter_tiles, tuple(range(groups)), early_tiles, quarter_tiles, tiles_here, lists,
        rows_buf, norms_buf, frames_buf, one_buf, two_buf, table_ref,
    )
    for tile in range(quarter_tiles):
        rows = frames_buf[pl.ds((early_tiles + tile) * TILE, TILE), :].astype(jnp.float32)
        finish(early_tiles + tile, tile, None, None, column_of(rows * rows))


def pick_kernel(plan_ref, part_0, part_1, part_2, part_3, first_ref, second_ref, every):
    member = lax.axis_index(frame_axis)
    piece = lax.axis_index(group_axis)
    blocks = first_ref.shape[0]
    parts = (part_0, part_1, part_2, part_3)
    quarter_tiles = blocks // len(parts)
    rows = part_0.shape[1]
    for slot, part in enumerate(parts):
        every[:, slot * rows : (slot + 1) * rows, :] = part[...]
    for place in range(blocks):
        tile = plan_ref[member * blocks + place]
        block_of = tile // blocks
        inside = tile - block_of * blocks
        part = inside // quarter_tiles
        row = jnp.bitwise_xor(part, piece) * rows + block_of * quarter_tiles + (inside - part * quarter_tiles)
        first_ref[pl.ds(place, 1), :] = every[0, pl.ds(row, 1), :]
        second_ref[pl.ds(place, 1), :] = every[1, pl.ds(row, 1), :]


def exchanged(number, distance):
    return [(at, at ^ distance) for at in range(number)]


def gathered_frames(frames, medoids, tile_ids, tile_counts, plan):
    width = frames.shape[1]
    blocks = frames.shape[0] // TILE
    members = lax.axis_size(frame_axis)
    groups = lax.axis_size(group_axis)
    rows = medoids[0]
    tile_rows = rows.shape[0]
    quarter_tiles = blocks // groups
    quarter = quarter_tiles * TILE
    side = tile_rows // TILE // 3 * TILE

    hbm = pl.BlockSpec(memory_space=pl.ANY)
    scalar = pl.BlockSpec(memory_space=pltpu.SMEM)
    vector = pl.BlockSpec(memory_space=pltpu.VMEM)
    small = pltpu.CompilerParams(vmem_limit_bytes=small_vmem)
    large = pltpu.CompilerParams(vmem_limit_bytes=large_vmem)
    mine, edge = pl.pallas_call(
        cut_first_kernel,
        out_shape=(
            jax.ShapeDtypeStruct((quarter, width), frames.dtype),
            jax.ShapeDtypeStruct((side, width), rows.dtype),
        ),
        in_specs=[hbm, hbm],
        out_specs=(vector, vector),
        scratch_shapes=[pltpu.SemaphoreType.DMA((2,))],
        compiler_params=pltpu.CompilerParams(vmem_limit_bytes=whole_vmem),
    )(frames, rows)
    inside_rows = pl.pallas_call(
        functools.partial(cut_middle_kernel, side),
        out_shape=jax.ShapeDtypeStruct((tile_rows - 2 * side, width), rows.dtype),
        in_specs=[hbm],
        out_specs=vector,
        scratch_shapes=[pltpu.SemaphoreType.DMA],
        compiler_params=small,
    )(rows)
    frames_2 = lax.ppermute(mine, frame_axis, exchanged(members, 2))
    frames_1 = lax.ppermute(mine, frame_axis, exchanged(members, 1))
    frames_3a = lax.ppermute(mine, frame_axis, [(1, 2), (2, 1)])
    frames_3b = lax.ppermute(frames_2, frame_axis, [(2, 3), (1, 0)])

    far_a = lax.ppermute(edge, group_axis, exchanged(groups, 2))
    far_b = lax.ppermute(inside_rows, group_axis, exchanged(groups, 2))
    far_c = lax.ppermute(far_a, slab_axis, exchanged(2, 1))
    near_group = lax.ppermute(rows, group_axis, exchanged(groups, 1))
    last_a = lax.ppermute(far_a, group_axis, exchanged(groups, 1))
    last_b = lax.ppermute(far_b, group_axis, exchanged(groups, 1))
    last_c = lax.ppermute(far_c, group_axis, exchanged(groups, 1))

    tiles_here = tile_rows // TILE
    listed = pl.pallas_call(
        functools.partial(split_kernel, members, tiles_here),
        out_shape=jax.ShapeDtypeStruct((blocks, TILE), jnp.int32),
        in_specs=[vector],
        out_specs=vector,
        compiler_params=small,
    )(jnp.concatenate([tile_ids[0], tile_counts[0][:, None]], axis=1))
    near_listed = lax.ppermute(listed, group_axis, exchanged(groups, 1))
    routed = pl.pallas_call(
        route_kernel,
        out_shape=jax.ShapeDtypeStruct((4 * quarter_tiles, TILE), jnp.int32),
        in_specs=[vector] * 2,
        out_specs=vector,
        compiler_params=small,
    )(listed, near_listed)
    near_lists = [lax.ppermute(routed, frame_axis, exchanged(members, at)) for at in (1, 2, 3)]
    far_lists = pl.pallas_call(
        stack_kernel,
        out_shape=jax.ShapeDtypeStruct((members, 2 * quarter_tiles, TILE), jnp.int32),
        in_specs=[vector] * 4,
        out_specs=vector,
        compiler_params=small,
    )(routed, *near_lists)
    far_lists = lax.ppermute(far_lists, group_axis, exchanged(groups, 2))
    norms = pl.pallas_call(
        functools.partial(norms_kernel, 0.5),
        out_shape=jax.ShapeDtypeStruct((tiles_here, TILE), jnp.float32),
        in_specs=[vector],
        out_specs=vector,
        compiler_params=small,
    )(rows)
    norm_near = lax.ppermute(norms, group_axis, exchanged(groups, 1))
    norm_pair = jnp.stack([norms, norm_near])
    norm_far = lax.ppermute(norm_pair, group_axis, exchanged(groups, 2))
    frame_norms = pl.pallas_call(
        functools.partial(norms_kernel, 1.0),
        out_shape=jax.ShapeDtypeStruct((3 * quarter_tiles, TILE), jnp.float32),
        in_specs=[vector] * 3,
        out_specs=vector,
        compiler_params=small,
    )(mine, frames_1, frames_2)

    total_tiles = members * quarter_tiles
    early_tiles = 3 * quarter_tiles
    table_size = early_tiles * (groups * tile_ids.shape[2] // unroll + 1) + together
    before_own = pl.pallas_call(
        functools.partial(own_kernel, members),
        out_shape=jax.ShapeDtypeStruct((2, quarter_tiles, TILE), jnp.float32),
        in_specs=[hbm] * 2 + [vector] * 2 + [hbm] * 2 + [vector],
        out_specs=vector,
        scratch_shapes=[
            pltpu.SMEM((2, blocks, TILE), jnp.int32),
            pltpu.VMEM((2 * tile_rows, width), jnp.bfloat16),
            pltpu.VMEM((2 * tiles_here + 8, TILE), jnp.float32),
            pltpu.VMEM((quarter, TILE), jnp.float32),
            pltpu.VMEM((quarter, TILE), jnp.float32),
            pltpu.SMEM((table_size,), jnp.int32),
            pltpu.SemaphoreType.DMA((4,)),
        ],
        compiler_params=large,
    )(listed, near_listed, norms, norm_near, rows, near_group, mine)
    before_near = pl.pallas_call(
        near_kernel,
        out_shape=jax.ShapeDtypeStruct((2, 2 * quarter_tiles, TILE), jnp.float32),
        in_specs=[hbm] * 2 + [vector] * 2 + [hbm] * 4,
        out_specs=vector,
        scratch_shapes=[
            pltpu.SMEM((members, 2 * quarter_tiles, TILE), jnp.int32),
            pltpu.VMEM((2 * tile_rows, width), jnp.bfloat16),
            pltpu.VMEM((3 * quarter, width), jnp.bfloat16),
            pltpu.VMEM((2 * tiles_here + 8, TILE), jnp.float32),
            pltpu.VMEM((2 * quarter, TILE), jnp.float32),
            pltpu.VMEM((2 * quarter, TILE), jnp.float32),
            pltpu.SMEM((table_size,), jnp.int32),
            pltpu.SemaphoreType.DMA((8,)),
        ],
        compiler_params=large,
    )(*near_lists[:2], norms, norm_near, rows, near_group, frames_1, frames_2)
    found = pl.pallas_call(
        far_kernel,
        out_shape=jax.ShapeDtypeStruct((2, total_tiles, TILE), jnp.float32),
        in_specs=[hbm] * 2 + [vector] * 6 + [hbm] * 13,
        out_specs=vector,
        scratch_shapes=[
            pltpu.SMEM((members, groups * quarter_tiles, TILE), jnp.int32),
            pltpu.VMEM((groups * tile_rows, width), jnp.bfloat16),
            pltpu.VMEM((members * quarter, width), jnp.bfloat16),
            pltpu.VMEM((groups * tiles_here + 8, TILE), jnp.float32),
            pltpu.VMEM((3 * quarter, TILE), jnp.float32),
            pltpu.VMEM((3 * quarter, TILE), jnp.float32),
            pltpu.SMEM((table_size,), jnp.int32),
            pltpu.SemaphoreType.DMA((20,)),
        ],
        compiler_params=large,
    )(
        near_lists[2], far_lists, norms, norm_near, norm_far, before_own, before_near, frame_norms, rows, near_group,
        far_a, far_b, far_c, last_a, last_b, last_c, mine, frames_1, frames_2, frames_3a, frames_3b,
    )

    one, two = found[0], found[1]
    for at in (1, 2, 3):
        other = lax.ppermute(found, frame_axis, exchanged(members, at))
        one, two = fold_two(one, two, other[0], other[1])
    merged = jnp.stack([one, two])
    parts = [merged] + [lax.ppermute(merged, group_axis, exchanged(groups, at)) for at in (1, 2, 3)]
    first, second = pl.pallas_call(
        pick_kernel,
        out_shape=(jax.ShapeDtypeStruct((blocks, TILE), jnp.float32),) * 2,
        in_specs=[scalar] + [vector] * 4,
        out_specs=(vector, vector),
        scratch_shapes=[pltpu.VMEM((2, groups * members * quarter_tiles, TILE), jnp.float32)],
        compiler_params=small,
    )(plan, *parts)
    return (first.reshape(-1), second.reshape(-1))


def solution(mesh):
    placed = (
        P((slab_axis, frame_axis), None),
        P(group_axis, frame_axis, None),
        P(group_axis, (slab_axis, frame_axis), None),
        P(group_axis, (slab_axis, frame_axis)),
        P(slab_axis),
    )

    def per_device(frames, medoids, tile_ids, tile_counts, plan):
        blocks = frames.shape[0] // TILE
        quarters = mesh.shape[frame_axis] == 4 and mesh.shape[group_axis] == 4 and mesh.shape[slab_axis] == 2
        tiles_here = medoids.shape[1] // TILE
        if quarters and blocks % 4 == 0 and 3 <= tiles_here < TILE // 4:
            return gathered_frames(frames, medoids, tile_ids, tile_counts, plan)
        return gathered_medoids(frames, medoids, tile_ids, tile_counts, plan)

    return jax.shard_map(
        per_device,
        mesh=mesh,
        in_specs=placed,
        out_specs=(P((slab_axis, frame_axis)), P((slab_axis, frame_axis))),
        check_vma=False,
    )
```
